32 devices in a mesh: ctx: 8 (over z, y), mp: 4 (over x, core).
Axes of the slice: x: 2, y: 2, z: 4, core: 2. Of those that a mesh axis runs over, the one named last changes fastest.
Arguments:
- q_in: bfloat16 [8192, 4096], P('ctx', 'mp'), may hold values from -6 to 6
- k_in: bfloat16 [8192, 4096], P('ctx', 'mp'), may hold values from -6 to 6
- v_in: bfloat16 [8192, 4096], P('ctx', 'mp'), may hold values from -6 to 6
- short_filter: float32 [3, 7, 4096], P(None, None, 'mp'), may hold values from -2 to 2
- taps: float32 [128, 4096], P(None, 'mp'), may hold values from -0.5 to 0.5
- residue: float32 [16, 4096], P(None, 'mp'), may hold values from -3 to 3
- rate: float32 [16, 4096], P(None, 'mp'), may hold values from 2.3692846e-06 to 0.033333335
- out_weight: bfloat16 [4096, 4096], P('mp', 'ctx'), may hold values from -0.09375 to 0.09375
Outputs:
- mixed: bfloat16 [8192, 4096], P('ctx', 'mp')
The draws below stay inside these ranges and needn't reach their ends.
All inputs are finite; a program needn't handle non-finite values.
Results may differ from the reference program's by a relative error of at most 0.0095.
Values may be sent and summed in bfloat16 or wider, within the bound.
A program may use at most 192 MiB of HBM per device.

```python
import math
import jax
import jax.numpy as jnp
from jax import lax

D = 4096
TOK_DEV = 1024
MODES = 16
SHORT_LEN = 7
MEDIUM_LEN = 128
SEQ = 8192
N_MP = 4


def levels(rng, extent, cuts, least, top_value):
    def one(position, parts):
        draws = jax.random.uniform(jax.random.fold_in(jax.random.fold_in(rng, 6), position), (parts,), jnp.float32, least / len(cuts), top_value / len(cuts))
        return jnp.repeat(jnp.exp(draws), extent[position] // parts).reshape((-1,) + (1,) * (len(extent) - position - 1))

    level = one(*cuts[0])
    for cut in cuts[1:]:
        level = level * one(*cut)
    return level


def bell_draw(rng, dims, scale, reach, cuts=(), dtype=jnp.bfloat16):
    values = scale * jax.random.normal(rng, dims, jnp.float32)
    if cuts:
        values = values * levels(rng, dims, cuts, -0.22, 0.18)
    return jnp.clip(values, -reach, reach).astype(dtype)


def setup_inputs(seed: int = 0) -> dict:
    streams_of = jax.random.split(jax.random.key(seed), 9)
    q_in = bell_draw(streams_of[0], (SEQ, D), 1.0, 6.0, ((0, 8), (1, 4)))
    k_in = bell_draw(streams_of[1], (SEQ, D), 1.0, 6.0, ((0, 8), (1, 4)))
    v_in = bell_draw(streams_of[2], (SEQ, D), 1.0, 6.0, ((0, 8), (1, 4)))
    short_filter = bell_draw(streams_of[3], (3, SHORT_LEN, D), SHORT_LEN ** -0.5, 2.0, ((2, 4),), jnp.float32)
    taps = bell_draw(streams_of[4], (MEDIUM_LEN, D), 0.08, 0.5, ((1, 4),), jnp.float32)
    residue = bell_draw(streams_of[5], (MODES, D), 0.5, 3.0, ((1, 4),), jnp.float32)
    rate = jnp.clip(jnp.exp(math.log(0.033333335) - 9.551725 * jax.random.uniform(streams_of[6], (MODES, D), jnp.float32) ** levels(streams_of[6], (MODES, D), ((1, 4),), -0.2, 0.2)), 2.3692846298217773e-06, 0.033333335)
    out_weight = bell_draw(streams_of[7], (D, D), D ** -0.5, 0.09375, ((0, 4), (1, 8)))
    return dict(q_in=q_in, k_in=k_in, v_in=v_in, short_filter=short_filter, taps=taps, residue=residue, rate=rate, out_weight=out_weight)


def causal_short(signal, filt_rows):
    values = signal.astype(jnp.float32)
    padded = jnp.pad(values, ((SHORT_LEN - 1, 0), (0, 0)))
    running = jnp.zeros_like(values)
    for offset in range(SHORT_LEN):
        first_row = SHORT_LEN - 1 - offset
        running = running + filt_rows[offset][None, :] * padded[first_row:first_row + SEQ]
    return running

def long_group(packed):
    signal, tap_cols, rate_cols, mode_cols = packed
    moments = jnp.arange(SEQ).astype(jnp.float32)[:, None]
    kernel = jnp.zeros(signal.shape, jnp.float32)
    for mode_idx in range(MODES):
        kernel = kernel + mode_cols[mode_idx][None, :] * jnp.exp(-rate_cols[mode_idx][None, :] * moments)
    kernel = kernel.at[:MEDIUM_LEN].add(tap_cols)
    length = 2 * SEQ
    spectrum = jnp.fft.rfft(signal, n=length, axis=0) * jnp.fft.rfft(kernel, n=length, axis=0)
    return jnp.fft.irfft(spectrum, n=length, axis=0)[:SEQ].astype(jnp.float32)

def reference(q_in, k_in, v_in, short_filter, taps, residue, rate, out_weight):
    q_short = causal_short(q_in, short_filter[0]).astype(jnp.bfloat16)
    gated_sig = (causal_short(k_in, short_filter[1]) * causal_short(v_in, short_filter[2])).astype(jnp.bfloat16)
    mode_weight = residue * jnp.sqrt(2.0 * rate)
    chan_group = min(D, 256)
    group_count = D // chan_group

    def split_cols(matrix):
        return matrix.reshape(matrix.shape[0], group_count, chan_group).transpose(1, 0, 2)
    outputs = lax.map(long_group, (split_cols(gated_sig.astype(jnp.float32)), split_cols(taps), split_cols(rate), split_cols(mode_weight)))
    long_conv = outputs.transpose(1, 0, 2).reshape(SEQ, D).astype(jnp.bfloat16)
    product = (q_short.astype(jnp.float32) * long_conv.astype(jnp.float32)).astype(jnp.bfloat16)
    chan_share = D // N_MP

    def project(tok_block):
        summed = jnp.zeros((tok_block.shape[0], D), jnp.float32)
        for shard_idx in range(N_MP):
            lo_col = shard_idx * chan_share
            part_sum = jnp.dot(tok_block[:, lo_col:lo_col + chan_share], out_weight[lo_col:lo_col + chan_share], preferred_element_type=jnp.float32)
            rounded = lax.optimization_barrier(part_sum.astype(jnp.bfloat16))
            summed = summed + rounded.astype(jnp.float32)
        return summed.astype(jnp.bfloat16)
    mixed = lax.map(project, product.reshape(SEQ // TOK_DEV, TOK_DEV, D))
    return mixed.reshape(SEQ, D)
```

```python
import functools

import jax
import jax.numpy as jnp
import numpy as np
from jax import lax
from jax.experimental import pallas as pl
from jax.experimental.pallas import tpu as pltpu
from jax.sharding import PartitionSpec as P

SHORT_LEN = 7
LANES = 128
LEAD = 8


def shifted(array, axis):
    peers = lax.axis_size(axis)
    return lax.ppermute(array, axis, [(i, i + 1) for i in range(peers - 1)])


def split_const(matrix):
    high = matrix.astype(jnp.bfloat16)
    low = (matrix - high.astype(np.float64)).astype(jnp.bfloat16)
    return jnp.asarray(np.stack([high, low]))


@functools.lru_cache
def dft_matrices(block):
    size = 2 * block
    freq = np.arange(block)[:, None]
    pos = np.arange(block)[None, :]
    angle = 2 * np.pi * ((freq * pos) % size) / size
    fwd = np.concatenate([np.cos(angle), -np.sin(angle)])
    fwd[block] = 1.0 - 2.0 * (np.arange(block) % 2)
    out_pos = block + np.arange(block)[:, None]
    freq = np.arange(block)[None, :]
    angle = 2 * np.pi * ((freq * out_pos) % size) / size
    real = 2 * np.cos(angle)
    imag = -2 * np.sin(angle)
    real[:, 0] = 1.0
    imag[:, 0] = 1.0 - 2.0 * (np.arange(block) % 2)
    inv = np.concatenate([real, imag], 1) / size
    return fwd, fwd[:, ::-1], inv


def mm(a, b):
    return jnp.dot(a, b, preferred_element_type=jnp.float32)


def mm_wide(pair, values):
    high = values.astype(jnp.bfloat16)
    low = (values - high.astype(jnp.float32)).astype(jnp.bfloat16)
    return mm(pair[0], high) + mm(pair[0], low) + mm(pair[1], high)


def spectrum_parts(spec, block, row0):
    real, imag = spec[:block], spec[block:]
    return real, jnp.where(row0, 0.0, imag), jnp.where(row0, imag, real)


def spectrum_mul(parts, spec, block):
    real, imag, cross = parts
    sr, si = spec[:block], spec[block:]
    return real * sr - imag * si, cross * si + imag * sr


def fill(scratch, lead_rows, signal):
    scratch[:LEAD] = lead_rows.astype(jnp.float32)
    scratch[LEAD:] = signal.astype(jnp.float32)


def short_taps(scratch, filt, start, block):
    total = filt[0:1] * scratch[LEAD + start : LEAD + start + block]
    for lag in range(1, SHORT_LEN):
        first = LEAD + start - lag
        total = total + filt[lag : lag + 1] * scratch[first : first + block]
    return total


def local_kernel(
    k_ref, v_ref, lead_ref, filt_ref, res_ref, rate_ref, gated_ref, h_rev_ref, ends_ref,
    state_ref, tail_ref, ks, vs, gs,
):
    block = h_rev_ref.shape[0]
    pieces = k_ref.shape[0] // block
    modes = rate_ref.shape[0]
    fill(ks, lead_ref[1], k_ref[...])
    fill(vs, lead_ref[2], v_ref[...])
    for b in range(pieces):
        gated = short_taps(ks, filt_ref[1], b * block, block) * short_taps(
            vs, filt_ref[2], b * block, block
        )
        rounded = gated.astype(jnp.bfloat16)
        gated_ref[b * block : (b + 1) * block] = rounded
        gs[b * block : (b + 1) * block] = rounded.astype(jnp.float32)
        if b == pieces - 1:
            tail_ref[...] = rounded
    rows = lax.broadcasted_iota(jnp.int32, (block, LANES), 0)
    back = (block - 1 - rows).astype(jnp.float32)

    def one_mode(n, h_rev):
        rate = rate_ref[pl.ds(n, 1), :]
        decay = jnp.exp(-rate * back)
        for b in range(pieces):
            ends_ref[n, b : b + 1, :] = jnp.sum(
                decay * gs[b * block : (b + 1) * block], axis=0, keepdims=True
            )
        return h_rev + (res_ref[pl.ds(n, 1), :] * jnp.sqrt(2.0 * rate)) * decay

    h_rev_ref[...] = lax.fori_loop(
        0, modes, one_mode, jnp.zeros((block, LANES), jnp.float32), unroll=2
    )

    step = jnp.exp(-rate_ref[...] * float(block))
    state = ends_ref[:, 0, :]
    for b in range(1, pieces):
        state = step * state + ends_ref[:, b, :]
    state_ref[...] = state


def block_kernel(
    peers, gated_ref, h_rev_ref, taps_ref, fwd_ref, rev_ref, inv_ref, states_ref, tail_ref,
    y_ref, all_ref, before_ref, landed, landed_tail, send, recv, tail_sems,
):
    index = pl.program_id(0)

    @pl.when(index == 0)
    def _():
        exchange_start(peers, states_ref, tail_ref, landed, landed_tail, send, recv, tail_sems)

    block = taps_ref.shape[0]
    pieces = gated_ref.shape[0] // block
    rows = lax.broadcasted_iota(jnp.int32, (block, LANES), 0)
    row0 = rows == 0
    sign = (1 - 2 * (rows % 2)).astype(jnp.float32)
    sign = jnp.concatenate([sign, sign], 0)
    taps_spec = mm_wide(fwd_ref, taps_ref[...])
    near_spec = sign * (taps_spec + mm_wide(rev_ref, h_rev_ref[...]))
    far = spectrum_parts(taps_spec, block, row0)
    near = spectrum_parts(near_spec, block, row0)
    previous = None
    for b in range(pieces):
        signal = gated_ref[b * block : (b + 1) * block]
        spec = mm(fwd_ref[0], signal) + mm(fwd_ref[1], signal)
        real, imag = spectrum_mul(near, spec, block)
        if previous is not None:
            more_real, more_imag = spectrum_mul(far, previous, block)
            real, imag = real + more_real, imag + more_imag
        y_ref[b * block : (b + 1) * block] = mm_wide(inv_ref, jnp.concatenate([real, imag], 0))
        previous = spec

    @pl.when(index == pl.num_programs(0) - 1)
    def _():
        exchange_finish(peers, states_ref, tail_ref, landed, landed_tail, send, recv, tail_sems)
        all_ref[...] = landed[...]
        before_ref[...] = landed_tail[...]


def finish_kernel(
    y_ref, ends_ref, start_ref, tail_ref, q_ref, lead_ref, filt_ref, taps_ref, res_ref, rate_ref,
    fwd_ref, inv_ref, out_ref, qs, lift, states,
):
    block = taps_ref.shape[0]
    pieces = q_ref.shape[0] // block
    modes = rate_ref.shape[0]
    fill(qs, lead_ref[0], q_ref[...])
    rows = lax.broadcasted_iota(jnp.int32, (block, LANES), 0)
    ahead = (rows + 1).astype(jnp.float32)
    for n in range(modes):
        rate = rate_ref[n : n + 1, :]
        lift[n] = (res_ref[n : n + 1, :] * jnp.sqrt(2.0 * rate)) * jnp.exp(-rate * ahead)
    step = jnp.exp(-rate_ref[...] * float(block))
    state = start_ref[...]
    states[0] = state
    for b in range(1, pieces):
        state = step * state + ends_ref[:, b - 1, :]
        states[b] = state
    taps_spec = mm_wide(fwd_ref, taps_ref[...])
    far = spectrum_parts(taps_spec, block, rows == 0)
    tail = tail_ref[...]
    spec = mm(fwd_ref[0], tail) + mm(fwd_ref[1], tail)
    halo = mm_wide(inv_ref, jnp.concatenate(spectrum_mul(far, spec, block), 0))
    for b in range(pieces):
        span = slice(b * block, (b + 1) * block)
        total = y_ref[span]
        if b == 0:
            total = total + halo
        for n in range(modes):
            total = total + lift[n] * states[b, n : n + 1, :]
        q_short = short_taps(qs, filt_ref[0], b * block, block).astype(jnp.bfloat16)
        long_conv = total.astype(jnp.bfloat16)
        out_ref[span] = (q_short.astype(jnp.float32) * long_conv.astype(jnp.float32)).astype(
            jnp.bfloat16
        )

MESH = pl.DeviceIdType.MESH


def tail_copy(peer, tail_ref, before_ref, tail_sems):
    return pltpu.make_async_remote_copy(
        src_ref=tail_ref, dst_ref=before_ref, send_sem=tail_sems.at[0],
        recv_sem=tail_sems.at[1], device_id={"ctx": peer}, device_id_type=MESH,
    )


def state_copy(peer, slot, hop, state_ref, all_ref, send, recv):
    return pltpu.make_async_remote_copy(
        src_ref=state_ref, dst_ref=all_ref.at[slot], send_sem=send.at[hop],
        recv_sem=recv.at[slot], device_id={"ctx": peer}, device_id_type=MESH,
    )


def exchange_start(peers, state_ref, tail_ref, all_ref, before_ref, send, recv, tail_sems):
    me = lax.axis_index("ctx")
    barrier = pltpu.get_barrier_semaphore()
    for hop in range(1, peers):
        pl.semaphore_signal(
            barrier, inc=1, device_id={"ctx": lax.rem(me + hop, peers)}, device_id_type=MESH
        )
    pl.semaphore_wait(barrier, peers - 1)

    @pl.when(me < peers - 1)
    def _():
        tail_copy(me + 1, tail_ref, before_ref, tail_sems).start()

    for hop in range(1, peers):
        state_copy(lax.rem(me + hop, peers), me, hop, state_ref, all_ref, send, recv).start()
    all_ref[me] = state_ref[...]

    @pl.when(me == 0)
    def _():
        before_ref[...] = jnp.zeros_like(before_ref)


def exchange_finish(peers, state_ref, tail_ref, all_ref, before_ref, send, recv, tail_sems):
    me = lax.axis_index("ctx")
    for hop in range(1, peers):
        source = lax.rem(me + hop, peers)
        state_copy(source, source, hop, state_ref, all_ref, send, recv).wait_recv()
        state_copy(source, me, hop, state_ref, all_ref, send, recv).wait_send()

    @pl.when(me > 0)
    def _():
        tail_copy(me, tail_ref, before_ref, tail_sems).wait_recv()

    @pl.when(me < peers - 1)
    def _():
        tail_copy(me + 1, tail_ref, before_ref, tail_sems).wait_send()


def project_kernel(
    prod_ref, w_ref, out_ref, near_out, near_in, far_out, far_in, mine_out, mine_in, hold, total,
    sems,
):
    me = lax.axis_index("mp")
    high, low = me // 2, lax.rem(me, 2)
    pair = high * 2 + (1 - low)
    across = (1 - high) * 2 + low
    chunks, rows, width = near_out.shape
    step = 256

    barrier = pltpu.get_barrier_semaphore()
    for peer in (pair, across):
        pl.semaphore_signal(barrier, inc=1, device_id={"mp": peer}, device_id_type=MESH)
    pl.semaphore_wait(barrier, 2)

    def copy(kind, t, source, target, peer):
        return pltpu.make_async_remote_copy(
            src_ref=source.at[t], dst_ref=target.at[t], send_sem=sems.at[2 * kind, t],
            recv_sem=sems.at[2 * kind + 1, t], device_id={"mp": peer}, device_id_type=MESH,
        )

    def near_copy(t):
        return copy(0, t, near_out, near_in, pair)

    def far_copy(t):
        return copy(1, t, far_out, far_in, across)

    def mine_copy(t):
        return copy(2, t, mine_out, mine_in, pair)

    def partial(t, owner, put):
        left = prod_ref[pl.ds(pl.multiple_of(t * rows, rows), rows), :]
        for col in range(0, width, step):
            first = pl.multiple_of(owner * width + col, step)
            put(col, mm(left, w_ref[:, pl.ds(first, step)]))

    def send_near(t):
        def put(col, value):
            near_out[t, :, col : col + step] = value.astype(jnp.bfloat16)

        partial(t, (1 - high) * 2 + (1 - low), put)
        near_copy(t).start()

        def keep(col, value):
            hold[t, :, col : col + step] = value

        partial(t, across, keep)

    def send_far(t):
        near_copy(t).wait_recv()
        far_out[t] = (hold[t] + near_in[t].astype(jnp.float32)).astype(jnp.bfloat16)
        far_copy(t).start()

    def first_pass(t, carry):
        send_near(t)

        @pl.when(t > 0)
        def _():
            send_far(t - 1)

        return carry

    lax.fori_loop(0, chunks, first_pass, 0)
    send_far(chunks - 1)

    def second_pass(t, carry):
        def put(col, value):
            mine_out[t, :, col : col + step] = value.astype(jnp.bfloat16)

        partial(t, pair, put)
        mine_copy(t).start()

        def keep(col, value):
            total[t, :, col : col + step] = value

        partial(t, me, keep)
        return carry

    lax.fori_loop(0, chunks, second_pass, 0)

    def finish(t, carry):
        mine_copy(t).wait_recv()
        far_copy(t).wait_recv()
        summed = total[t] + mine_in[t].astype(jnp.float32) + far_in[t].astype(jnp.float32)
        out_ref[pl.ds(pl.multiple_of(t * rows, rows), rows), :] = summed.astype(jnp.bfloat16)
        near_copy(t).wait_send()
        far_copy(t).wait_send()
        mine_copy(t).wait_send()
        return carry

    lax.fori_loop(0, chunks, finish, 0)


def project(product, weight):
    tokens = product.shape[0]
    width = weight.shape[1] // lax.axis_size("mp")
    chunks = 8
    box = (chunks, tokens // chunks, width)
    vmem = pl.BlockSpec(memory_space=pltpu.VMEM)
    return pl.pallas_call(
        project_kernel,
        in_specs=[vmem] * 2,
        out_specs=vmem,
        out_shape=jax.ShapeDtypeStruct((tokens, width), jnp.bfloat16),
        scratch_shapes=[pltpu.VMEM(box, jnp.bfloat16)] * 6
        + [pltpu.VMEM(box, jnp.float32)] * 2
        + [pltpu.SemaphoreType.DMA((6, chunks))],
        compiler_params=pltpu.CompilerParams(
            collective_id=1, has_side_effects=True, vmem_limit_bytes=48 << 20
        ),
        name="project",
    )(product, weight)


def ring_place(chip, count):
    odd = chip % 2
    return (chip // 2) * (1 - odd) + (count - 1 - chip // 2) * odd


def ring_chip(place, count):
    back = place // (count // 2)
    return 2 * place * (1 - back) + (2 * (count - 1 - place) + 1) * back


LEAD_ROWS = 16
CHUNKS = 4


def spread(rows):
    return jnp.stack([jnp.broadcast_to(rows[n : n + 1], (8, LANES)) for n in range(rows.shape[0])])


def packed_product(near, spec, far, previous):
    block = spec.shape[0] // 2
    nr, ni, sr, si = near[:block], near[block:], spec[:block], spec[block:]
    fr, fi, pr, pi = far[:block], far[block:], previous[:block], previous[block:]
    real = (nr * sr - ni * si) + (fr * pr - fi * pi)
    imag = (nr * si + ni * sr) + (fr * pi + fi * pr)
    row0 = lax.broadcasted_iota(jnp.int32, (8, LANES), 0) == 0
    real_top = jnp.where(row0, nr[:8] * sr[:8] + fr[:8] * pr[:8], real[:8])
    imag_top = jnp.where(row0, ni[:8] * si[:8] + fi[:8] * pi[:8], imag[:8])
    return jnp.concatenate([real_top, real[8:], imag_top, imag[8:]], 0)


def fused_kernel(
    peers, q_ref, k_ref, v_ref, w_ref, filt_ref, taps_ref, res_ref, rate_ref, fwd3_ref, fwd2_ref,
    inv_ref, out_ref, qbuf, kbuf, vbuf, ks, vs, gbuf, before, hold, ends_ref, state_ref, all_ref,
    start_ref, near_ref, far_ref, y_ref, prod_ref, ring, pair_out, pair_in, cross_out, cross_in,
    kept, load_sems, own_sems, halo_sems, tail_sems, state_send, state_recv, ring_sems, pair_sems,
    cross_sems,
):
    tokens, chans = prod_ref.shape
    block = taps_ref.shape[0]
    pieces = tokens // block
    modes = rate_ref.shape[0]
    blocks = chans // LANES
    f32, bf16 = jnp.float32, jnp.bfloat16
    ctx = lax.axis_index("ctx")
    me = lax.axis_index("mp")
    high, low = me // 2, lax.rem(me, 2)
    pair = high * 2 + (1 - low)
    across = (1 - high) * 2 + low
    place = ring_place(ctx, peers)

    def neighbour(offset):
        return ring_chip(lax.rem(place + offset + peers, peers), peers)

    ahead, behind = neighbour(1), neighbour(-1)

    loads = [
        pltpu.make_async_copy(src, dst.at[pl.ds(LEAD_ROWS, tokens)], load_sems.at[n])
        for n, (src, dst) in enumerate(((k_ref, kbuf), (v_ref, vbuf), (q_ref, qbuf)))
    ]
    owns = [
        pltpu.make_async_copy(
            w_ref.at[:, pl.ds(k * LANES, LANES)], ring.at[ctx, k], own_sems.at[k]
        )
        for k in range(CHUNKS)
    ]
    for copy in owns + loads:
        copy.start()

    barrier = pltpu.get_barrier_semaphore()
    for hop in range(1, peers):
        pl.semaphore_signal(
            barrier, inc=1, device_id={"ctx": lax.rem(ctx + hop, peers)}, device_id_type=MESH
        )
    for peer in (pair, across):
        pl.semaphore_signal(barrier, inc=1, device_id={"mp": peer}, device_id_type=MESH)
    pl.semaphore_wait(barrier, peers + 1)

    def halo_copy(n, src, dst, peer):
        return pltpu.make_async_remote_copy(
            src_ref=src.at[pl.ds(tokens - LEAD_ROWS, LEAD_ROWS)], dst_ref=dst.at[pl.ds(0, LEAD_ROWS)],
            send_sem=halo_sems.at[0, n], recv_sem=halo_sems.at[1, n],
            device_id={"ctx": peer}, device_id_type=MESH,
        )

    halos = ((k_ref, kbuf), (v_ref, vbuf), (q_ref, qbuf))

    @pl.when(ctx < peers - 1)
    def _():
        for n, (src, dst) in enumerate(halos):
            halo_copy(n, src, dst, ctx + 1).start()

    def ring_copy(way, seq, chip, k):
        return pltpu.make_async_remote_copy(
            src_ref=ring.at[chip, k], dst_ref=ring.at[chip, k],
            send_sem=ring_sems.at[2 * way, seq], recv_sem=ring_sems.at[2 * way + 1, seq],
            device_id={"ctx": behind if way else ahead}, device_id_type=MESH,
        )

    for k in range(CHUNKS):
        owns[k].wait()
        for way in (0, 1):
            ring_copy(way, k, ctx, k).start()

    def chunk_at(seq, way):
        hop = seq // CHUNKS
        chip = neighbour(hop + 1 if way else -hop - 1)
        return chip, seq % CHUNKS + 2 * way * (hop // 3)

    def arrive(seq):
        for way in (0, 1):
            chip, k = chunk_at(seq, way)
            ring_copy(way, seq, chip, k).wait_recv()

            @pl.when(seq < 8 + 2 * (1 - way))
            def _():
                ring_copy(way, seq + CHUNKS, chip, k).start()

            if way:
                @pl.when((seq >= 10) & (seq < 12))
                def _():
                    ring_copy(way, seq + 2, chip, k).start()

    @pl.when(ctx == 0)
    def _():
        for _, dst in halos:
            dst[0:LEAD_ROWS] = jnp.zeros((LEAD_ROWS, chans), bf16)
        before[...] = jnp.zeros_like(before)

    def halo_wait(n):
        @pl.when(ctx > 0)
        def _():
            halo_copy(n, *halos[n], ctx).wait_recv()

    def lanes(i):
        return pl.ds(pl.multiple_of(i * LANES, LANES), LANES)

    def short(scratch, branch, b, col):
        first = LEAD_ROWS + b * block
        total = filt_ref[branch, 0:1, col] * scratch[first : first + block]
        for lag in range(1, SHORT_LEN):
            total = total + filt_ref[branch, lag : lag + 1, col] * scratch[
                first - lag : first - lag + block
            ]
        return total

    sub = lax.broadcasted_iota(jnp.int32, (8, LANES), 0).astype(f32)

    for n in (0, 1):
        loads[n].wait()
        halo_wait(n)

    def gate_body(i, carry):
        col = lanes(i)
        ks[...] = kbuf[:, col].astype(f32)
        vs[...] = vbuf[:, col].astype(f32)
        rate = rate_ref[:, col]
        d8 = spread(jnp.exp(-8.0 * rate))
        last = jnp.exp(-spread(rate) * (7.0 - sub)[None])
        acc = jnp.zeros((modes, 8, LANES), f32)
        for b in range(pieces):
            gated = short(ks, 1, b, col) * short(vs, 2, b, col)
            rounded = gated.astype(bf16)
            gbuf[b * block : (b + 1) * block, col] = rounded
            back = rounded.astype(f32)
            for r in range(block // 8):
                acc = acc * d8 + back[8 * r : 8 * r + 8][None]
            hold[b] = (acc * last).reshape(modes * 8, LANES)
        for b in range(pieces):
            ends = hold[b, pl.ds(0, modes, stride=8), :]
            for j in range(1, 8):
                ends = ends + hold[b, pl.ds(j, modes, stride=8), :]
            ends_ref[b, :, col] = ends
            if b == pieces - 1:
                state_ref[:, col] = ends
        return carry

    lax.fori_loop(0, blocks, gate_body, 0)

    def tail_copy(peer):
        return pltpu.make_async_remote_copy(
            src_ref=gbuf.at[pl.ds(tokens - block, block)], dst_ref=before,
            send_sem=tail_sems.at[0], recv_sem=tail_sems.at[1],
            device_id={"ctx": peer}, device_id_type=MESH,
        )

    def state_copy(peer, slot, hop):
        return pltpu.make_async_remote_copy(
            src_ref=state_ref, dst_ref=all_ref.at[slot], send_sem=state_send.at[hop],
            recv_sem=state_recv.at[slot], device_id={"ctx": peer}, device_id_type=MESH,
        )

    @pl.when(ctx < peers - 1)
    def _():
        tail_copy(ctx + 1).start()

    for hop in range(1, peers):
        @pl.when(ctx + hop < peers)
        def _():
            state_copy(ctx + hop, ctx, hop).start()

    arrive(0)
    arrive(1)

    sign = (1 - 2 * (lax.broadcasted_iota(jnp.int32, (2 * block, LANES), 0) % 2)).astype(f32)

    def spectrum(*signals):
        both = jnp.concatenate(signals, 1)
        return mm(fwd2_ref[...], jnp.concatenate([both, both], 0))

    def conv_body(i, carry):
        col = lanes(i)
        rate = rate_ref[:, col]
        d8 = spread(jnp.exp(-8.0 * rate))
        u = spread(res_ref[:, col] * jnp.sqrt(2.0 * rate)) * jnp.exp(-spread(rate) * sub[None])
        rows = []
        for r in range(block // 8):
            rows.append(jnp.sum(u, axis=0))
            if r < block // 8 - 1:
                u = u * d8
        taps = taps_ref[:, col]
        values = jnp.concatenate([taps, taps + jnp.concatenate(rows, 0)], 1)
        top = values.astype(bf16)
        rest = (values - top.astype(f32)).astype(bf16)
        filters = mm(fwd3_ref[...], jnp.concatenate([top, rest, top], 0))
        far_ref[:, col] = filters[:, :LANES]
        near_ref[:, col] = sign * filters[:, LANES:]
        previous = None
        waiting = []
        for b in range(0, pieces, 2):
            both = spectrum(
                gbuf[b * block : (b + 1) * block, col], gbuf[(b + 1) * block : (b + 2) * block, col]
            )
            for half in (0, 1):
                spec = both[:, half * LANES : (half + 1) * LANES]
                if previous is not None:
                    waiting.append(
                        packed_product(near_ref[:, col], spec, far_ref[:, col], previous).astype(bf16)
                    )
                previous = spec
                done = b + half
                if len(waiting) == 2 or (waiting and done == pieces - 1):
                    count = len(waiting)
                    y = mm(inv_ref[...], jnp.concatenate(waiting, 1))
                    for n in range(count):
                        at = (done - count + 1 + n) * block
                        y_ref[at : at + block, col] = y[:, n * LANES : (n + 1) * LANES]
                    waiting = []
        return carry

    lax.fori_loop(0, blocks, conv_body, 0)

    arrive(2)
    arrive(3)

    loads[2].wait()
    halo_wait(2)

    @pl.when(ctx > 0)
    def _():
        tail_copy(ctx).wait_recv()

    for hop in range(1, peers):
        @pl.when(ctx - hop >= 0)
        def _():
            state_copy(ctx, ctx - hop, hop).wait_recv()

    def carry_state(p, state):
        return state * jnp.exp(-rate_ref[...] * float(tokens)) + all_ref[p]

    start_ref[...] = lax.fori_loop(0, ctx, carry_state, jnp.zeros((modes, chans), f32))

    def finish_body(i, carry):
        col = lanes(i)
        ks[...] = qbuf[:, col].astype(f32)
        both = spectrum(before[:, col], gbuf[0:block, col])
        first = packed_product(
            near_ref[:, col], both[:, LANES:], far_ref[:, col], both[:, :LANES]
        ).astype(bf16)
        y0 = mm(inv_ref[...], first)
        rate = rate_ref[:, col]
        d8 = spread(jnp.exp(-8.0 * rate))
        lift = spread(res_ref[:, col] * jnp.sqrt(2.0 * rate)) * jnp.exp(
            -spread(rate) * (sub + 1.0)[None]
        )
        step = jnp.exp(-rate * float(block))
        base = start_ref[:, col]
        for b in range(pieces):
            at = slice(b * block, (b + 1) * block)
            state = base
            if b > 0:
                base = base * step
                state = base + ends_ref[b - 1, :, col]
            u = lift * spread(state)
            rows = []
            for r in range(block // 8):
                rows.append(jnp.sum(u, axis=0))
                if r < block // 8 - 1:
                    u = u * d8
            near = y0 if b == 0 else y_ref[at, col]
            long_conv = (near + jnp.concatenate(rows, 0)).astype(bf16)
            q_short = short(ks, 0, b, col).astype(bf16)
            prod_ref[at, col] = (q_short.astype(f32) * long_conv.astype(f32)).astype(bf16)
        return carry

    lax.fori_loop(0, blocks, finish_body, 0)

    events = 2 + 3 * CHUNKS + CHUNKS // 2
    row_step = 256

    def chunk_of(t, side):
        own = 1 - (t + 14) // 16
        seq = (t - 2) * (1 - own)
        chip, k = chunk_at(seq, side)
        return own * ctx + (1 - own) * chip, own * (2 * t + side) + (1 - own) * k

    def role(chip, k):
        owner = chip // 2
        gap = owner // 2 - high
        cross = gap * gap
        sub_slot = lax.rem(chip, 2) * CHUNKS + k
        return lax.rem(owner, 2) == low, cross, (owner // 2) * 2 * CHUNKS + sub_slot, sub_slot

    def pair_copy(slot):
        return pltpu.make_async_remote_copy(
            src_ref=pair_out.at[slot], dst_ref=pair_in.at[slot], send_sem=pair_sems.at[0, slot],
            recv_sem=pair_sems.at[1, slot], device_id={"mp": pair}, device_id_type=MESH,
        )

    def cross_copy(slot):
        return pltpu.make_async_remote_copy(
            src_ref=cross_out.at[slot], dst_ref=cross_in.at[slot], send_sem=cross_sems.at[0, slot],
            recv_sem=cross_sems.at[1, slot], device_id={"mp": across}, device_id_type=MESH,
        )

    def settle(t):
        for side in (0, 1):
            mine, cross, slot, sub_slot = role(*chunk_of(t, side))

            @pl.when(mine & (cross == 1))
            def _():
                pair_copy(slot).wait_recv()
                cross_out[sub_slot] = (kept[slot] + pair_in[slot].astype(f32)).astype(bf16)
                cross_copy(sub_slot).start()

    def event(t, carry):
        @pl.when(t >= 2 + CHUNKS)
        def _():
            arrive(t - 2)

        spots = [chunk_of(t, side) for side in (0, 1)]
        roles = [role(*spot) for spot in spots]

        def products(r, carry):
            at = pl.ds(pl.multiple_of(r * row_step, row_step), row_step)
            right = jnp.concatenate([ring[chip, k] for chip, k in spots], 1)
            value = mm(prod_ref[at, :], right)
            for side in (0, 1):
                mine, _, slot, _ = roles[side]
                part = value[:, side * LANES : (side + 1) * LANES]

                @pl.when(mine)
                def _():
                    kept[slot, at, :] = part

                @pl.when(jnp.logical_not(mine))
                def _():
                    pair_out[slot, at, :] = part.astype(bf16)

            return carry

        lax.fori_loop(0, tokens // row_step, products, 0)
        for mine, _, slot, _ in roles:
            @pl.when(jnp.logical_not(mine))
            def _():
                pair_copy(slot).start()

        @pl.when(t > 0)
        def _():
            settle(t - 1)

        return carry

    lax.fori_loop(0, events, event, 0)
    settle(events - 1)

    def finish(n, carry):
        slot = high * 2 * CHUNKS + n
        pair_copy(slot).wait_recv()
        cross_copy(n).wait_recv()
        total = kept[slot] + pair_in[slot].astype(f32) + cross_in[n].astype(f32)
        out_ref[:, lanes(n)] = total.astype(bf16)
        return carry

    lax.fori_loop(0, 2 * CHUNKS, finish, 0)

    def drain(n, carry):
        pair_copy((1 - low) * 0 + n).wait_send()
        return carry

    lax.fori_loop(0, 4 * CHUNKS, drain, 0)
    for n in range(2 * CHUNKS):
        cross_copy(n).wait_send()
    for way in (0, 1):
        for seq in range(3 * CHUNKS + CHUNKS // 2):
            ring_copy(way, seq, ctx, 0).wait_send()

    @pl.when(ctx < peers - 1)
    def _():
        for n, (src, dst) in enumerate(halos):
            halo_copy(n, src, dst, ctx + 1).wait_send()
        tail_copy(ctx + 1).wait_send()

    for hop in range(1, peers):
        @pl.when(ctx + hop < peers)
        def _():
            state_copy(ctx + hop, ctx, hop).wait_send()


def fused(q_in, k_in, v_in, short_filter, taps, residue, rate, out_weight):
    tokens, chans = q_in.shape
    block = taps.shape[0]
    modes = rate.shape[0]
    pieces = tokens // block
    peers = lax.axis_size("ctx")
    f32, bf16 = jnp.float32, jnp.bfloat16
    fwd, _, inv = dft_matrices(block)
    high = fwd.astype(jnp.bfloat16)
    low = (fwd - high.astype(np.float64)).astype(jnp.bfloat16)
    fwd3 = jnp.asarray(np.concatenate([high, high, low], 1))
    fwd2 = jnp.asarray(np.concatenate([high, low], 1))
    inv1 = jnp.asarray(inv.astype(jnp.bfloat16))
    vmem = pl.BlockSpec(memory_space=pltpu.VMEM)
    hbm = pl.BlockSpec(memory_space=pl.ANY)
    padded = (LEAD_ROWS + tokens, chans)
    narrow = (LEAD_ROWS + tokens, LANES)
    dma = pltpu.SemaphoreType.DMA
    return pl.pallas_call(
        functools.partial(fused_kernel, peers),
        in_specs=[hbm] * 4 + [vmem] * 7,
        out_specs=vmem,
        out_shape=jax.ShapeDtypeStruct((tokens, chans), bf16),
        scratch_shapes=[pltpu.VMEM(padded, bf16)] * 3
        + [pltpu.VMEM(narrow, f32)] * 2
        + [
            pltpu.VMEM((tokens, chans), bf16),
            pltpu.VMEM((block, chans), bf16),
            pltpu.VMEM((pieces, modes * 8, LANES), f32),
            pltpu.VMEM((pieces, modes, chans), f32),
            pltpu.VMEM((modes, chans), f32),
            pltpu.VMEM((peers, modes, chans), f32),
            pltpu.VMEM((modes, chans), f32),
            pltpu.VMEM((2 * block, chans), f32),
            pltpu.VMEM((2 * block, chans), f32),
            pltpu.VMEM((tokens, chans), f32),
            pltpu.VMEM((tokens, chans), bf16),
            pltpu.VMEM((peers, CHUNKS, chans, LANES), bf16),
            pltpu.VMEM((4 * CHUNKS, tokens, LANES), bf16),
            pltpu.VMEM((4 * CHUNKS, tokens, LANES), bf16),
            pltpu.VMEM((2 * CHUNKS, tokens, LANES), bf16),
            pltpu.VMEM((2 * CHUNKS, tokens, LANES), bf16),
            pltpu.VMEM((4 * CHUNKS, tokens, LANES), f32),
            dma((3,)), dma((CHUNKS,)), dma((2, 3)), dma((2,)), dma((peers,)), dma((peers,)),
            dma((4, 4 * CHUNKS)), dma((2, 4 * CHUNKS)), dma((2, 2 * CHUNKS)),
        ],
        compiler_params=pltpu.CompilerParams(
            collective_id=2, has_side_effects=True, vmem_limit_bytes=60 << 20
        ),
        name="fused",
    )(q_in, k_in, v_in, out_weight, short_filter, taps, residue, rate, fwd3, fwd2, inv1)


def cols(*lead):
    return pl.BlockSpec(lead + (LANES,), lambda i: (0,) * len(lead) + (i,))


def whole(shape):
    return pl.BlockSpec(shape, lambda i: (0,) * len(shape))


def local(q_in, k_in, v_in, short_filter, taps, residue, rate, out_weight):
    tokens, chans = q_in.shape
    block = taps.shape[0]
    modes = rate.shape[0]
    pieces = tokens // block
    columns = out_weight.shape[1]
    if (lax.axis_size("ctx"), lax.axis_size("mp"), columns) == (8, 4, CHUNKS * LANES):
        return fused(q_in, k_in, v_in, short_filter, taps, residue, rate, out_weight)
    fwd, rev, inv = [split_const(m) for m in dft_matrices(block)]
    grid = (chans // LANES,)
    f32, bf16 = jnp.float32, jnp.bfloat16
    lead = shifted(jnp.stack([q_in[-LEAD:], k_in[-LEAD:], v_in[-LEAD:]]), "ctx")
    filt_spec = cols(3, SHORT_LEN)
    params = pltpu.CompilerParams(vmem_limit_bytes=62 << 20)
    gated, h_rev, ends, state, tail = pl.pallas_call(
        local_kernel,
        grid=grid,
        in_specs=[
            cols(tokens), cols(tokens), cols(3, LEAD), filt_spec, cols(modes), cols(modes),
        ],
        out_specs=[cols(tokens), cols(block), cols(modes, pieces), cols(modes), cols(block)],
        out_shape=[
            jax.ShapeDtypeStruct((tokens, chans), bf16),
            jax.ShapeDtypeStruct((block, chans), f32),
            jax.ShapeDtypeStruct((modes, pieces, chans), f32),
            jax.ShapeDtypeStruct((modes, chans), f32),
            jax.ShapeDtypeStruct((block, chans), bf16),
        ],
        scratch_shapes=[
            pltpu.VMEM((LEAD + tokens, LANES), f32),
            pltpu.VMEM((LEAD + tokens, LANES), f32),
            pltpu.VMEM((tokens, LANES), f32),
        ],
        compiler_params=params,
        name="gate",
    )(k_in, v_in, lead, short_filter, residue, rate)

    peers = lax.axis_size("ctx")
    all_shape = (peers,) + state.shape
    y_part, all_states, before = pl.pallas_call(
        functools.partial(block_kernel, peers),
        grid=grid,
        in_specs=[
            cols(tokens), cols(block), cols(block), whole(fwd.shape), whole(rev.shape),
            whole(inv.shape), whole(state.shape), whole(tail.shape),
        ],
        out_specs=[cols(tokens), whole(all_shape), whole(tail.shape)],
        out_shape=[
            jax.ShapeDtypeStruct((tokens, chans), f32),
            jax.ShapeDtypeStruct(all_shape, f32),
            jax.ShapeDtypeStruct(tail.shape, bf16),
        ],
        scratch_shapes=[
            pltpu.VMEM(all_shape, f32),
            pltpu.VMEM(tail.shape, bf16),
            pltpu.SemaphoreType.DMA((peers,)),
            pltpu.SemaphoreType.DMA((peers,)),
            pltpu.SemaphoreType.DMA((2,)),
        ],
        compiler_params=pltpu.CompilerParams(
            collective_id=0, has_side_effects=True, vmem_limit_bytes=62 << 20
        ),
        name="block_conv",
    )(gated, h_rev, taps, fwd, rev, inv, state, tail)
    gap = lax.axis_index("ctx") - 1 - jnp.arange(all_states.shape[0])
    spans = (jnp.maximum(gap, 0) * tokens).astype(f32)[:, None, None]
    carried = jnp.where((gap >= 0)[:, None, None], jnp.exp(-rate[None] * spans) * all_states, 0.0)
    start = jnp.sum(carried, axis=0)

    product = pl.pallas_call(
        finish_kernel,
        grid=grid,
        in_specs=[
            cols(tokens), cols(modes, pieces), cols(modes), cols(block), cols(tokens),
            cols(3, LEAD), filt_spec, cols(block), cols(modes), cols(modes),
            whole(fwd.shape), whole(inv.shape),
        ],
        out_specs=cols(tokens),
        out_shape=jax.ShapeDtypeStruct((tokens, chans), bf16),
        scratch_shapes=[
            pltpu.VMEM((LEAD + tokens, LANES), f32),
            pltpu.VMEM((modes, block, LANES), f32),
            pltpu.VMEM((pieces, modes, LANES), f32),
        ],
        compiler_params=params,
        name="finish_conv",
    )(y_part, ends, start, before, q_in, lead, short_filter, taps, residue, rate, fwd, inv)

    return project(product, lax.all_gather(out_weight, "ctx", axis=1, tiled=True))


def solution(mesh):
    in_specs = (
        P("ctx", "mp"),
        P("ctx", "mp"),
        P("ctx", "mp"),
        P(None, None, "mp"),
        P(None, "mp"),
        P(None, "mp"),
        P(None, "mp"),
        P("mp", "ctx"),
    )
    out_specs = P("ctx", "mp")
    return jax.shard_map(local, mesh=mesh, in_specs=in_specs, out_specs=out_specs, check_vma=False)
```

```python
import functools

import jax
import jax.numpy as jnp
import numpy as np
from jax import lax
from jax.experimental import pallas as pl
from jax.experimental.pallas import tpu as pltpu
from jax.sharding import PartitionSpec as P

SHORT_LEN = 7
LANES = 128
LEAD = 8


def shifted(array, axis):
    peers = lax.axis_size(axis)
    return lax.ppermute(array, axis, [(i, i + 1) for i in range(peers - 1)])


def split_const(matrix):
    high = matrix.astype(jnp.bfloat16)
    low = (matrix - high.astype(np.float64)).astype(jnp.bfloat16)
    return jnp.asarray(np.stack([high, low]))


@functools.lru_cache
def dft_matrices(block):
    size = 2 * block
    freq = np.arange(block)[:, None]
    pos = np.arange(block)[None, :]
    angle = 2 * np.pi * ((freq * pos) % size) / size
    fwd = np.concatenate([np.cos(angle), -np.sin(angle)])
    fwd[block] = 1.0 - 2.0 * (np.arange(block) % 2)
    out_pos = block + np.arange(block)[:, None]
    freq = np.arange(block)[None, :]
    angle = 2 * np.pi * ((freq * out_pos) % size) / size
    real = 2 * np.cos(angle)
    imag = -2 * np.sin(angle)
    real[:, 0] = 1.0
    imag[:, 0] = 1.0 - 2.0 * (np.arange(block) % 2)
    inv = np.concatenate([real, imag], 1) / size
    return fwd, fwd[:, ::-1], inv


def mm(a, b):
    return jnp.dot(a, b, preferred_element_type=jnp.float32)


def mm_wide(pair, values):
    high = values.astype(jnp.bfloat16)
    low = (values - high.astype(jnp.float32)).astype(jnp.bfloat16)
    return mm(pair[0], high) + mm(pair[0], low) + mm(pair[1], high)


def spectrum_parts(spec, block, row0):
    real, imag = spec[:block], spec[block:]
    return real, jnp.where(row0, 0.0, imag), jnp.where(row0, imag, real)


def spectrum_mul(parts, spec, block):
    real, imag, cross = parts
    sr, si = spec[:block], spec[block:]
    return real * sr - imag * si, cross * si + imag * sr


def fill(scratch, lead_rows, signal):
    scratch[:LEAD] = lead_rows.astype(jnp.float32)
    scratch[LEAD:] = signal.astype(jnp.float32)


def short_taps(scratch, filt, start, block):
    total = filt[0:1] * scratch[LEAD + start : LEAD + start + block]
    for lag in range(1, SHORT_LEN):
        first = LEAD + start - lag
        total = total + filt[lag : lag + 1] * scratch[first : first + block]
    return total


def local_kernel(
    k_ref, v_ref, lead_ref, filt_ref, res_ref, rate_ref, gated_ref, h_rev_ref, ends_ref,
    state_ref, tail_ref, ks, vs, gs,
):
    block = h_rev_ref.shape[0]
    pieces = k_ref.shape[0] // block
    modes = rate_ref.shape[0]
    fill(ks, lead_ref[1], k_ref[...])
    fill(vs, lead_ref[2], v_ref[...])
    for b in range(pieces):
        gated = short_taps(ks, filt_ref[1], b * block, block) * short_taps(
            vs, filt_ref[2], b * block, block
        )
        rounded = gated.astype(jnp.bfloat16)
        gated_ref[b * block : (b + 1) * block] = rounded
        gs[b * block : (b + 1) * block] = rounded.astype(jnp.float32)
        if b == pieces - 1:
            tail_ref[...] = rounded
    rows = lax.broadcasted_iota(jnp.int32, (block, LANES), 0)
    back = (block - 1 - rows).astype(jnp.float32)

    def one_mode(n, h_rev):
        rate = rate_ref[pl.ds(n, 1), :]
        decay = jnp.exp(-rate * back)
        for b in range(pieces):
            ends_ref[n, b : b + 1, :] = jnp.sum(
                decay * gs[b * block : (b + 1) * block], axis=0, keepdims=True
            )
        return h_rev + (res_ref[pl.ds(n, 1), :] * jnp.sqrt(2.0 * rate)) * decay

    h_rev_ref[...] = lax.fori_loop(
        0, modes, one_mode, jnp.zeros((block, LANES), jnp.float32), unroll=2
    )

    step = jnp.exp(-rate_ref[...] * float(block))
    state = ends_ref[:, 0, :]
    for b in range(1, pieces):
        state = step * state + ends_ref[:, b, :]
    state_ref[...] = state


def block_kernel(
    peers, gated_ref, h_rev_ref, taps_ref, fwd_ref, rev_ref, inv_ref, states_ref, tail_ref,
    y_ref, all_ref, before_ref, landed, landed_tail, send, recv, tail_sems,
):
    index = pl.program_id(0)

    @pl.when(index == 0)
    def _():
        exchange_start(peers, states_ref, tail_ref, landed, landed_tail, send, recv, tail_sems)

    block = taps_ref.shape[0]
    pieces = gated_ref.shape[0] // block
    rows = lax.broadcasted_iota(jnp.int32, (block, LANES), 0)
    row0 = rows == 0
    sign = (1 - 2 * (rows % 2)).astype(jnp.float32)
    sign = jnp.concatenate([sign, sign], 0)
    taps_spec = mm_wide(fwd_ref, taps_ref[...])
    near_spec = sign * (taps_spec + mm_wide(rev_ref, h_rev_ref[...]))
    far = spectrum_parts(taps_spec, block, row0)
    near = spectrum_parts(near_spec, block, row0)
    previous = None
    for b in range(pieces):
        signal = gated_ref[b * block : (b + 1) * block]
        spec = mm(fwd_ref[0], signal) + mm(fwd_ref[1], signal)
        real, imag = spectrum_mul(near, spec, block)
        if previous is not None:
            more_real, more_imag = spectrum_mul(far, previous, block)
            real, imag = real + more_real, imag + more_imag
        y_ref[b * block : (b + 1) * block] = mm_wide(inv_ref, jnp.concatenate([real, imag], 0))
        previous = spec

    @pl.when(index == pl.num_programs(0) - 1)
    def _():
        exchange_finish(peers, states_ref, tail_ref, landed, landed_tail, send, recv, tail_sems)
        all_ref[...] = landed[...]
        before_ref[...] = landed_tail[...]


def finish_kernel(
    y_ref, ends_ref, start_ref, tail_ref, q_ref, lead_ref, filt_ref, taps_ref, res_ref, rate_ref,
    fwd_ref, inv_ref, out_ref, qs, lift, states,
):
    block = taps_ref.shape[0]
    pieces = q_ref.shape[0] // block
    modes = rate_ref.shape[0]
    fill(qs, lead_ref[0], q_ref[...])
    rows = lax.broadcasted_iota(jnp.int32, (block, LANES), 0)
    ahead = (rows + 1).astype(jnp.float32)
    for n in range(modes):
        rate = rate_ref[n : n + 1, :]
        lift[n] = (res_ref[n : n + 1, :] * jnp.sqrt(2.0 * rate)) * jnp.exp(-rate * ahead)
    step = jnp.exp(-rate_ref[...] * float(block))
    state = start_ref[...]
    states[0] = state
    for b in range(1, pieces):
        state = step * state + ends_ref[:, b - 1, :]
        states[b] = state
    taps_spec = mm_wide(fwd_ref, taps_ref[...])
    far = spectrum_parts(taps_spec, block, rows == 0)
    tail = tail_ref[...]
    spec = mm(fwd_ref[0], tail) + mm(fwd_ref[1], tail)
    halo = mm_wide(inv_ref, jnp.concatenate(spectrum_mul(far, spec, block), 0))
    for b in range(pieces):
        span = slice(b * block, (b + 1) * block)
        total = y_ref[span]
        if b == 0:
            total = total + halo
        for n in range(modes):
            total = total + lift[n] * states[b, n : n + 1, :]
        q_short = short_taps(qs, filt_ref[0], b * block, block).astype(jnp.bfloat16)
        long_conv = total.astype(jnp.bfloat16)
        out_ref[span] = (q_short.astype(jnp.float32) * long_conv.astype(jnp.float32)).astype(
            jnp.bfloat16
        )

MESH = pl.DeviceIdType.MESH


def tail_copy(peer, tail_ref, before_ref, tail_sems):
    return pltpu.make_async_remote_copy(
        src_ref=tail_ref, dst_ref=before_ref, send_sem=tail_sems.at[0],
        recv_sem=tail_sems.at[1], device_id={"ctx": peer}, device_id_type=MESH,
    )


def state_copy(peer, slot, hop, state_ref, all_ref, send, recv):
    return pltpu.make_async_remote_copy(
        src_ref=state_ref, dst_ref=all_ref.at[slot], send_sem=send.at[hop],
        recv_sem=recv.at[slot], device_id={"ctx": peer}, device_id_type=MESH,
    )


def exchange_start(peers, state_ref, tail_ref, all_ref, before_ref, send, recv, tail_sems):
    me = lax.axis_index("ctx")
    barrier = pltpu.get_barrier_semaphore()
    for hop in range(1, peers):
        pl.semaphore_signal(
            barrier, inc=1, device_id={"ctx": lax.rem(me + hop, peers)}, device_id_type=MESH
        )
    pl.semaphore_wait(barrier, peers - 1)

    @pl.when(me < peers - 1)
    def _():
        tail_copy(me + 1, tail_ref, before_ref, tail_sems).start()

    for hop in range(1, peers):
        state_copy(lax.rem(me + hop, peers), me, hop, state_ref, all_ref, send, recv).start()
    all_ref[me] = state_ref[...]

    @pl.when(me == 0)
    def _():
        before_ref[...] = jnp.zeros_like(before_ref)


def exchange_finish(peers, state_ref, tail_ref, all_ref, before_ref, send, recv, tail_sems):
    me = lax.axis_index("ctx")
    for hop in range(1, peers):
        source = lax.rem(me + hop, peers)
        state_copy(source, source, hop, state_ref, all_ref, send, recv).wait_recv()
        state_copy(source, me, hop, state_ref, all_ref, send, recv).wait_send()

    @pl.when(me > 0)
    def _():
        tail_copy(me, tail_ref, before_ref, tail_sems).wait_recv()

    @pl.when(me < peers - 1)
    def _():
        tail_copy(me + 1, tail_ref, before_ref, tail_sems).wait_send()


def project_kernel(
    prod_ref, w_ref, out_ref, near_out, near_in, far_out, far_in, mine_out, mine_in, hold, total,
    sems,
):
    me = lax.axis_index("mp")
    high, low = me // 2, lax.rem(me, 2)
    pair = high * 2 + (1 - low)
    across = (1 - high) * 2 + low
    chunks, rows, width = near_out.shape
    step = 256

    barrier = pltpu.get_barrier_semaphore()
    for peer in (pair, across):
        pl.semaphore_signal(barrier, inc=1, device_id={"mp": peer}, device_id_type=MESH)
    pl.semaphore_wait(barrier, 2)

    def copy(kind, t, source, target, peer):
        return pltpu.make_async_remote_copy(
            src_ref=source.at[t], dst_ref=target.at[t], send_sem=sems.at[2 * kind, t],
            recv_sem=sems.at[2 * kind + 1, t], device_id={"mp": peer}, device_id_type=MESH,
        )

    def near_copy(t):
        return copy(0, t, near_out, near_in, pair)

    def far_copy(t):
        return copy(1, t, far_out, far_in, across)

    def mine_copy(t):
        return copy(2, t, mine_out, mine_in, pair)

    def partial(t, owner, put):
        left = prod_ref[pl.ds(pl.multiple_of(t * rows, rows), rows), :]
        for col in range(0, width, step):
            first = pl.multiple_of(owner * width + col, step)
            put(col, mm(left, w_ref[:, pl.ds(first, step)]))

    def send_near(t):
        def put(col, value):
            near_out[t, :, col : col + step] = value.astype(jnp.bfloat16)

        partial(t, (1 - high) * 2 + (1 - low), put)
        near_copy(t).start()

        def keep(col, value):
            hold[t, :, col : col + step] = value

        partial(t, across, keep)

    def send_far(t):
        near_copy(t).wait_recv()
        far_out[t] = (hold[t] + near_in[t].astype(jnp.float32)).astype(jnp.bfloat16)
        far_copy(t).start()

    def first_pass(t, carry):
        send_near(t)

        @pl.when(t > 0)
        def _():
            send_far(t - 1)

        return carry

    lax.fori_loop(0, chunks, first_pass, 0)
    send_far(chunks - 1)

    def second_pass(t, carry):
        def put(col, value):
            mine_out[t, :, col : col + step] = value.astype(jnp.bfloat16)

        partial(t, pair, put)
        mine_copy(t).start()

        def keep(col, value):
            total[t, :, col : col + step] = value

        partial(t, me, keep)
        return carry

    lax.fori_loop(0, chunks, second_pass, 0)

    def finish(t, carry):
        mine_copy(t).wait_recv()
        far_copy(t).wait_recv()
        summed = total[t] + mine_in[t].astype(jnp.float32) + far_in[t].astype(jnp.float32)
        out_ref[pl.ds(pl.multiple_of(t * rows, rows), rows), :] = summed.astype(jnp.bfloat16)
        near_copy(t).wait_send()
        far_copy(t).wait_send()
        mine_copy(t).wait_send()
        return carry

    lax.fori_loop(0, chunks, finish, 0)


def project(product, weight):
    tokens = product.shape[0]
    width = weight.shape[1] // lax.axis_size("mp")
    chunks = 8
    box = (chunks, tokens // chunks, width)
    vmem = pl.BlockSpec(memory_space=pltpu.VMEM)
    return pl.pallas_call(
        project_kernel,
        in_specs=[vmem] * 2,
        out_specs=vmem,
        out_shape=jax.ShapeDtypeStruct((tokens, width), jnp.bfloat16),
        scratch_shapes=[pltpu.VMEM(box, jnp.bfloat16)] * 6
        + [pltpu.VMEM(box, jnp.float32)] * 2
        + [pltpu.SemaphoreType.DMA((6, chunks))],
        compiler_params=pltpu.CompilerParams(
            collective_id=1, has_side_effects=True, vmem_limit_bytes=48 << 20
        ),
        name="project",
    )(product, weight)


def ring_place(chip, count):
    odd = chip % 2
    return (chip // 2) * (1 - odd) + (count - 1 - chip // 2) * odd


def ring_chip(place, count):
    back = place // (count // 2)
    return 2 * place * (1 - back) + (2 * (count - 1 - place) + 1) * back


LEAD_ROWS = 16
CHUNKS = 4


def spread(rows):
    return jnp.stack([jnp.broadcast_to(rows[n : n + 1], (8, LANES)) for n in range(rows.shape[0])])


def packed_product(near, spec, far, previous):
    block = spec.shape[0] // 2
    nr, ni, sr, si = near[:block], near[block:], spec[:block], spec[block:]
    fr, fi, pr, pi = far[:block], far[block:], previous[:block], previous[block:]
    real = (nr * sr - ni * si) + (fr * pr - fi * pi)
    imag = (nr * si + ni * sr) + (fr * pi + fi * pr)
    row0 = lax.broadcasted_iota(jnp.int32, (8, LANES), 0) == 0
    real_top = jnp.where(row0, nr[:8] * sr[:8] + fr[:8] * pr[:8], real[:8])
    imag_top = jnp.where(row0, ni[:8] * si[:8] + fi[:8] * pi[:8], imag[:8])
    return jnp.concatenate([real_top, real[8:], imag_top, imag[8:]], 0)


def fused_kernel(
    peers, q_ref, k_ref, v_ref, w_ref, filt_ref, taps_ref, res_ref, rate_ref, fwd3_ref, fwd2_ref,
    inv_ref, out_ref, qbuf, kbuf, vbuf, ks, vs, gbuf, before, hold, ends_ref, state_ref, peer_ref,
    prefix_ref, onward_ref, start_ref, near_ref, far_ref, y_ref, prod_ref, ring, part, pair_in,
    cross_out, cross_in, load_sems, own_sems, halo_sems, tail_sems, state_sems, ring_sems,
    pair_sems, cross_sems,
):
    tokens, chans = prod_ref.shape
    block = taps_ref.shape[0]
    pieces = tokens // block
    modes = rate_ref.shape[0]
    blocks = chans // LANES
    f32, bf16 = jnp.float32, jnp.bfloat16
    ctx = lax.axis_index("ctx")
    me = lax.axis_index("mp")
    high, low = me // 2, lax.rem(me, 2)
    pair = high * 2 + (1 - low)
    across = (1 - high) * 2 + low
    place = ring_place(ctx, peers)

    def neighbour(offset):
        return ring_chip(lax.rem(place + offset + peers, peers), peers)

    ahead, behind = neighbour(1), neighbour(-1)

    loads = [
        pltpu.make_async_copy(src, dst.at[pl.ds(LEAD_ROWS, tokens)], load_sems.at[n])
        for n, (src, dst) in enumerate(((k_ref, kbuf), (v_ref, vbuf), (q_ref, qbuf)))
    ]
    owns = [
        pltpu.make_async_copy(
            w_ref.at[:, pl.ds(k * LANES, LANES)], ring.at[ctx, k], own_sems.at[k]
        )
        for k in range(CHUNKS)
    ]
    for copy in owns + loads:
        copy.start()

    barrier = pltpu.get_barrier_semaphore()
    for hop in range(1, peers):
        pl.semaphore_signal(
            barrier, inc=1, device_id={"ctx": lax.rem(ctx + hop, peers)}, device_id_type=MESH
        )
    for peer in (pair, across):
        pl.semaphore_signal(barrier, inc=1, device_id={"mp": peer}, device_id_type=MESH)
    pl.semaphore_wait(barrier, peers + 1)

    def halo_copy(n, src, dst, peer):
        return pltpu.make_async_remote_copy(
            src_ref=src.at[pl.ds(tokens - LEAD_ROWS, LEAD_ROWS)], dst_ref=dst.at[pl.ds(0, LEAD_ROWS)],
            send_sem=halo_sems.at[0, n], recv_sem=halo_sems.at[1, n],
            device_id={"ctx": peer}, device_id_type=MESH,
        )

    halos = ((k_ref, kbuf), (v_ref, vbuf), (q_ref, qbuf))

    @pl.when(ctx < peers - 1)
    def _():
        for n, (src, dst) in enumerate(halos):
            halo_copy(n, src, dst, ctx + 1).start()

    def ring_copy(way, seq, chip, k):
        return pltpu.make_async_remote_copy(
            src_ref=ring.at[chip, k], dst_ref=ring.at[chip, k],
            send_sem=ring_sems.at[2 * way, seq], recv_sem=ring_sems.at[2 * way + 1, seq],
            device_id={"ctx": behind if way else ahead}, device_id_type=MESH,
        )

    def send_own(k):
        for way in (0, 1):
            ring_copy(way, k, ctx, k).start()

    for copy in owns:
        copy.wait()
    send_own(0)
    send_own(1)

    def chunk_at(seq, way):
        hop = seq // CHUNKS
        chip = neighbour(hop + 1 if way else -hop - 1)
        return chip, seq % CHUNKS + 2 * way * (hop // 3)

    def arrive(seq):
        for way in (0, 1):
            chip, k = chunk_at(seq, way)
            ring_copy(way, seq, chip, k).wait_recv()

            @pl.when(seq < 8 + 2 * (1 - way))
            def _():
                ring_copy(way, seq + CHUNKS, chip, k).start()

            if way:
                @pl.when((seq >= 10) & (seq < 12))
                def _():
                    ring_copy(way, seq + 2, chip, k).start()

    @pl.when(ctx == 0)
    def _():
        for _, dst in halos:
            dst[0:LEAD_ROWS] = jnp.zeros((LEAD_ROWS, chans), bf16)
        before[...] = jnp.zeros_like(before)

    def halo_wait(n):
        @pl.when(ctx > 0)
        def _():
            halo_copy(n, *halos[n], ctx).wait_recv()

    def lanes(i):
        return pl.ds(pl.multiple_of(i * LANES, LANES), LANES)

    def short(scratch, branch, b, col):
        first = LEAD_ROWS + b * block
        total = filt_ref[branch, 0:1, col] * scratch[first : first + block]
        for lag in range(1, SHORT_LEN):
            total = total + filt_ref[branch, lag : lag + 1, col] * scratch[
                first - lag : first - lag + block
            ]
        return total

    sub = lax.broadcasted_iota(jnp.int32, (8, LANES), 0).astype(f32)

    for n in (0, 1):
        loads[n].wait()
        halo_wait(n)

    row, side_y = ctx // 2, lax.rem(ctx, 2)
    partner = ctx + 1 - 2 * side_y

    halves = 2
    part_blocks = blocks // halves

    def half(h):
        width = chans // halves
        return pl.ds(pl.multiple_of(h * width, width), width)

    def tail_copy(peer):
        return pltpu.make_async_remote_copy(
            src_ref=gbuf.at[pl.ds(tokens - block, block)], dst_ref=before, send_sem=tail_sems.at[0], recv_sem=tail_sems.at[1],
            device_id={"ctx": peer}, device_id_type=MESH,
        )

    def state_copy(h):
        return pltpu.make_async_remote_copy(
            src_ref=state_ref.at[:, half(h)], dst_ref=peer_ref.at[:, half(h)],
            send_sem=state_sems.at[0, h], recv_sem=state_sems.at[1, h],
            device_id={"ctx": partner}, device_id_type=MESH,
        )

    def prefix_copy(peer, h):
        return pltpu.make_async_remote_copy(
            src_ref=onward_ref.at[:, half(h)], dst_ref=prefix_ref.at[:, half(h)],
            send_sem=state_sems.at[2, h], recv_sem=state_sems.at[3, h],
            device_id={"ctx": peer}, device_id_type=MESH,
        )

    def gate_body(i, carry):
        col = lanes(i)
        ks[...] = kbuf[:, col].astype(f32)
        vs[...] = vbuf[:, col].astype(f32)
        rate = rate_ref[:, col]
        d8 = spread(jnp.exp(-8.0 * rate))
        last = jnp.exp(-spread(rate) * (7.0 - sub)[None])
        acc = jnp.zeros((modes, 8, LANES), f32)
        for b in range(pieces):
            gated = short(ks, 1, b, col) * short(vs, 2, b, col)
            rounded = gated.astype(bf16)
            gbuf[b * block : (b + 1) * block, col] = rounded
            back = rounded.astype(f32)
            for r in range(block // 8):
                acc = acc * d8 + back[8 * r : 8 * r + 8][None]
            hold[b] = (acc * last).reshape(modes * 8, LANES)
        for b in range(pieces):
            ends = hold[b, pl.ds(0, modes, stride=8), :]
            for j in range(1, 8):
                ends = ends + hold[b, pl.ds(j, modes, stride=8), :]
            ends_ref[b, :, col] = ends
            if b == pieces - 1:
                state_ref[:, col] = ends

        @pl.when(lax.rem(i, part_blocks) == part_blocks - 1)
        def _():
            state_copy(i // part_blocks).start()

        @pl.when(i == blocks - 2)
        def _():
            send_own(2)

        return carry

    lax.fori_loop(0, blocks, gate_body, 0)

    def chain(j):
        col = half(j)
        state_copy(j).wait_recv()
        decay = jnp.exp(-rate_ref[:, col] * float(tokens))
        mine, other = state_ref[:, col], peer_ref[:, col]
        first = jnp.where(side_y == 0, mine, other)
        second = jnp.where(side_y == 0, other, mine)

        @pl.when(row > 0)
        def _():
            prefix_copy(ctx, j).wait_recv()

        @pl.when(row == 0)
        def _():
            prefix_ref[:, col] = jnp.zeros((modes, chans // halves), f32)

        prefix = prefix_ref[:, col]
        between = prefix * decay + first

        @pl.when(row < peers // 2 - 1)
        def _():
            onward_ref[:, col] = between * decay + second
            prefix_copy(ctx + 2, j).start()

        start_ref[:, col] = jnp.where(side_y == 0, prefix, between)

    def chain_at(place_in_order):
        h = place_in_order - row

        @pl.when((h >= 0) & (h < halves))
        def _():
            chain(h)

        @pl.when((h == halves - 1) & (row < peers // 2 - 1))
        def _():
            tail_copy(ctx + 1).start()

    chain_at(0)

    sign = (1 - 2 * (lax.broadcasted_iota(jnp.int32, (2 * block, LANES), 0) % 2)).astype(f32)

    def spectrum(*signals):
        both = jnp.concatenate(signals, 1)
        return mm(fwd2_ref[...], jnp.concatenate([both, both], 0))

    def conv_body(i, carry):
        col = lanes(i)
        rate = rate_ref[:, col]
        d8 = spread(jnp.exp(-8.0 * rate))
        u = spread(res_ref[:, col] * jnp.sqrt(2.0 * rate)) * jnp.exp(-spread(rate) * sub[None])
        rows = []
        for r in range(block // 8):
            rows.append(jnp.sum(u, axis=0))
            if r < block // 8 - 1:
                u = u * d8
        taps = taps_ref[:, col]
        values = jnp.concatenate([taps, taps + jnp.concatenate(rows, 0)], 1)
        top = values.astype(bf16)
        rest = (values - top.astype(f32)).astype(bf16)
        filters = mm(fwd3_ref[...], jnp.concatenate([top, rest, top], 0))
        far_ref[:, col] = filters[:, :LANES]
        near_ref[:, col] = sign * filters[:, LANES:]
        previous = None
        waiting = []
        for b in range(0, pieces, 2):
            both = spectrum(
                gbuf[b * block : (b + 1) * block, col], gbuf[(b + 1) * block : (b + 2) * block, col]
            )
            for half in (0, 1):
                spec = both[:, half * LANES : (half + 1) * LANES]
                if previous is not None:
                    waiting.append(
                        packed_product(near_ref[:, col], spec, far_ref[:, col], previous).astype(bf16)
                    )
                previous = spec
                done = b + half
                if len(waiting) == 2 or (waiting and done == pieces - 1):
                    count = len(waiting)
                    y = mm(inv_ref[...], jnp.concatenate(waiting, 1))
                    for n in range(count):
                        at = (done - count + 1 + n) * block
                        y_ref[at : at + block, col] = y[:, n * LANES : (n + 1) * LANES]
                    waiting = []

        @pl.when(i == 1)
        def _():
            send_own(3)

        for seq in (0, 1):
            @pl.when(i == blocks - 2 + seq)
            def _():
                arrive(seq)

        @pl.when((i == 2) & (ctx == peers - 2))
        def _():
            tail_copy(ctx + 1).start()

        for n in (1, 2):
            @pl.when(i == 3 * n - 1)
            def _():
                chain_at(n)

        return carry

    lax.fori_loop(0, blocks, conv_body, 0)

    chain_at(3)

    loads[2].wait()
    halo_wait(2)

    def finish_piece(b, near, state, lift, d8, col):
        u = lift * spread(state)
        rows = []
        for r in range(block // 8):
            rows.append(jnp.sum(u, axis=0))
            if r < block // 8 - 1:
                u = u * d8
        long_conv = (near + jnp.concatenate(rows, 0)).astype(bf16)
        q_short = short(ks, 0, b, col).astype(bf16)
        prod_ref[b * block : (b + 1) * block, col] = (
            q_short.astype(f32) * long_conv.astype(f32)
        ).astype(bf16)

    def lifts(col):
        rate = rate_ref[:, col]
        lift = spread(res_ref[:, col] * jnp.sqrt(2.0 * rate)) * jnp.exp(
            -spread(rate) * (sub + 1.0)[None]
        )
        return lift, spread(jnp.exp(-8.0 * rate))

    def finish_body(i, carry):
        col = lanes(i)

        @pl.when(i == part_blocks)
        def _():
            chain_at(4)
            arrive(2)

        ks[...] = qbuf[:, col].astype(f32)
        lift, d8 = lifts(col)
        step = jnp.exp(-rate_ref[:, col] * float(block))
        base = start_ref[:, col]
        for b in range(1, pieces):
            base = base * step
            near = y_ref[b * block : (b + 1) * block, col]
            finish_piece(b, near, base + ends_ref[b - 1, :, col], lift, d8, col)
        return carry

    lax.fori_loop(0, blocks, finish_body, 0)

    @pl.when(ctx > 0)
    def _():
        tail_copy(ctx).wait_recv()

    def first_body(i, carry):
        col = lanes(i)
        first = LEAD_ROWS + block
        ks[:first] = qbuf[:first, col].astype(f32)
        both = spectrum(before[:, col], gbuf[0:block, col])
        spec = packed_product(
            near_ref[:, col], both[:, LANES:], far_ref[:, col], both[:, :LANES]
        ).astype(bf16)
        lift, d8 = lifts(col)
        finish_piece(0, mm(inv_ref[...], spec), start_ref[:, col], lift, d8, col)
        return carry

    lax.fori_loop(0, blocks, first_body, 0)

    arrive(3)

    events = 2 + 3 * CHUNKS + CHUNKS // 2
    row_step = 256
    strips = tokens // row_step

    def chunk_of(t, side):
        own = 1 - (t + 14) // 16
        seq = (t - 2) * (1 - own)
        chip, k = chunk_at(seq, side)
        return own * ctx + (1 - own) * chip, own * (2 * t + side) + (1 - own) * k

    def role(chip, k):
        owner = chip // 2
        gap = owner // 2 - high
        cross = gap * gap
        sub_slot = lax.rem(chip, 2) * CHUNKS + k
        return lax.rem(owner, 2) == low, cross, (owner // 2) * 2 * CHUNKS + sub_slot, sub_slot

    def pair_copy(chip, k, slot, r):
        at = pl.ds(pl.multiple_of(r * row_step, row_step), row_step)
        return pltpu.make_async_remote_copy(
            src_ref=part.at[chip, k, at], dst_ref=pair_in.at[slot, at],
            send_sem=pair_sems.at[0, slot * strips + r], recv_sem=pair_sems.at[1, slot * strips + r],
            device_id={"mp": pair}, device_id_type=MESH,
        )

    def cross_copy(slot, r):
        at = pl.ds(pl.multiple_of(r * row_step, row_step), row_step)
        return pltpu.make_async_remote_copy(
            src_ref=cross_out.at[slot, at], dst_ref=cross_in.at[slot, at],
            send_sem=cross_sems.at[0, slot * strips + r],
            recv_sem=cross_sems.at[1, slot * strips + r],
            device_id={"mp": across}, device_id_type=MESH,
        )

    def settle(spots, roles, r):
        at = pl.ds(pl.multiple_of(r * row_step, row_step), row_step)
        for (chip, k), (mine, cross, slot, sub_slot) in zip(spots, roles):
            @pl.when(mine & (cross == 1))
            def _():
                pair_copy(chip, k, slot, r).wait_recv()
                total = part[chip, k, at, :].astype(f32) + pair_in[slot, at, :].astype(f32)
                cross_out[sub_slot, at, :] = total.astype(bf16)
                cross_copy(sub_slot, r).start()

    def total(n):
        slot = high * 2 * CHUNKS + n
        chip, k = 2 * me + n // CHUNKS, n % CHUNKS
        for r in range(strips):
            pair_copy(chip, k, slot, r).wait_recv()
            cross_copy(n, r).wait_recv()
        value = part[chip, k].astype(f32) + pair_in[slot].astype(f32) + cross_in[n].astype(f32)
        out_ref[:, n * LANES : (n + 1) * LANES] = value.astype(bf16)

    def time_of(n):
        gap = lax.rem(ring_place(2 * me + n // CHUNKS, peers) - place + peers, peers)
        own, far = 1 - (gap + peers - 1) // peers, gap // (peers // 2)
        hop = (1 - far) * (gap - 1) + far * (peers - 1 - gap)
        k = n % CHUNKS
        return own * (k // 2) + (1 - own) * (2 + CHUNKS * hop + k - 2 * (hop // 3) * (k // 2))

    def event(t, carry):
        for n in range(3):
            @pl.when(t == 2 * n)
            def _():
                arrive(CHUNKS + n)

        @pl.when(t >= 5 + CHUNKS)
        def _():
            arrive(t - 2)

        spots = [chunk_of(t, side) for side in (0, 1)]
        roles = [role(*spot) for spot in spots]

        def products(r, carry):
            at = pl.ds(pl.multiple_of(r * row_step, row_step), row_step)
            right = jnp.concatenate([ring[chip, k] for chip, k in spots], 1)
            value = mm(prod_ref[at, :], right).astype(bf16)
            for n, ((chip, k), (mine, _, slot, _)) in enumerate(zip(spots, roles)):
                part[chip, k, at, :] = value[:, n * LANES : (n + 1) * LANES]

                @pl.when(jnp.logical_not(mine))
                def _():
                    pair_copy(chip, k, slot, r).start()

            @pl.when(r > 0)
            def _():
                settle(spots, roles, r - 1)

            return carry

        lax.fori_loop(0, strips, products, 0)
        settle(spots, roles, strips - 1)
        return carry

    early = events - 4
    lax.fori_loop(0, events - 1, event, 0)
    for n in range(2 * CHUNKS):
        @pl.when(time_of(n) <= early)
        def _():
            total(n)

    lax.fori_loop(events - 1, events, event, 0)
    for n in range(2 * CHUNKS):
        @pl.when(time_of(n) > early)
        def _():
            total(n)

    for n in range(4 * CHUNKS):
        for r in range(strips):
            pair_copy(0, 0, n, r).wait_send()
    for n in range(2 * CHUNKS):
        for r in range(strips):
            cross_copy(n, r).wait_send()
    for way in (0, 1):
        for seq in range(3 * CHUNKS + CHUNKS // 2):
            ring_copy(way, seq, ctx, 0).wait_send()

    @pl.when(ctx < peers - 1)
    def _():
        for n, (src, dst) in enumerate(halos):
            halo_copy(n, src, dst, ctx + 1).wait_send()
        tail_copy(ctx + 1).wait_send()

    for j in range(halves):
        state_copy(j).wait_send()

    @pl.when(row < peers // 2 - 1)
    def _():
        for j in range(halves):
            prefix_copy(ctx + 2, j).wait_send()


def fused(q_in, k_in, v_in, short_filter, taps, residue, rate, out_weight):
    tokens, chans = q_in.shape
    block = taps.shape[0]
    modes = rate.shape[0]
    pieces = tokens // block
    peers = lax.axis_size("ctx")
    f32, bf16 = jnp.float32, jnp.bfloat16
    fwd, _, inv = dft_matrices(block)
    high = fwd.astype(jnp.bfloat16)
    low = (fwd - high.astype(np.float64)).astype(jnp.bfloat16)
    fwd3 = jnp.asarray(np.concatenate([high, high, low], 1))
    fwd2 = jnp.asarray(np.concatenate([high, low], 1))
    inv1 = jnp.asarray(inv.astype(jnp.bfloat16))
    vmem = pl.BlockSpec(memory_space=pltpu.VMEM)
    hbm = pl.BlockSpec(memory_space=pl.ANY)
    padded = (LEAD_ROWS + tokens, chans)
    narrow = (LEAD_ROWS + tokens, LANES)
    dma = pltpu.SemaphoreType.DMA
    return pl.pallas_call(
        functools.partial(fused_kernel, peers),
        in_specs=[hbm] * 4 + [vmem] * 7,
        out_specs=vmem,
        out_shape=jax.ShapeDtypeStruct((tokens, chans), bf16),
        scratch_shapes=[pltpu.VMEM(padded, bf16)] * 3
        + [pltpu.VMEM(narrow, f32)] * 2
        + [
            pltpu.VMEM((tokens, chans), bf16),
            pltpu.VMEM((block, chans), bf16),
            pltpu.VMEM((pieces, modes * 8, LANES), f32),
            pltpu.VMEM((pieces, modes, chans), f32),
            pltpu.VMEM((modes, chans), f32),
            pltpu.VMEM((modes, chans), f32),
            pltpu.VMEM((modes, chans), f32),
            pltpu.VMEM((modes, chans), f32),
            pltpu.VMEM((modes, chans), f32),
            pltpu.VMEM((2 * block, chans), f32),
            pltpu.VMEM((2 * block, chans), f32),
            pltpu.VMEM((tokens, chans), f32),
            pltpu.VMEM((tokens, chans), bf16),
            pltpu.VMEM((peers, CHUNKS, chans, LANES), bf16),
            pltpu.VMEM((peers, CHUNKS, tokens, LANES), bf16),
            pltpu.VMEM((4 * CHUNKS, tokens, LANES), bf16),
            pltpu.VMEM((2 * CHUNKS, tokens, LANES), bf16),
            pltpu.VMEM((2 * CHUNKS, tokens, LANES), bf16),
            dma((3,)), dma((CHUNKS,)), dma((2, 3)), dma((2,)), dma((4, 2)),
            dma((4, 4 * CHUNKS)),
            dma((2, 4 * CHUNKS * (tokens // 256))), dma((2, 2 * CHUNKS * (tokens // 256))),
        ],
        compiler_params=pltpu.CompilerParams(
            collective_id=2, has_side_effects=True, vmem_limit_bytes=60 << 20
        ),
        name="fused",
    )(q_in, k_in, v_in, out_weight, short_filter, taps, residue, rate, fwd3, fwd2, inv1)


def cols(*lead):
    return pl.BlockSpec(lead + (LANES,), lambda i: (0,) * len(lead) + (i,))


def whole(shape):
    return pl.BlockSpec(shape, lambda i: (0,) * len(shape))


def local(q_in, k_in, v_in, short_filter, taps, residue, rate, out_weight):
    tokens, chans = q_in.shape
    block = taps.shape[0]
    modes = rate.shape[0]
    pieces = tokens // block
    columns = out_weight.shape[1]
    if (lax.axis_size("ctx"), lax.axis_size("mp"), columns) == (8, 4, CHUNKS * LANES):
        return fused(q_in, k_in, v_in, short_filter, taps, residue, rate, out_weight)
    fwd, rev, inv = [split_const(m) for m in dft_matrices(block)]
    grid = (chans // LANES,)
    f32, bf16 = jnp.float32, jnp.bfloat16
    lead = shifted(jnp.stack([q_in[-LEAD:], k_in[-LEAD:], v_in[-LEAD:]]), "ctx")
    filt_spec = cols(3, SHORT_LEN)
    params = pltpu.CompilerParams(vmem_limit_bytes=62 << 20)
    gated, h_rev, ends, state, tail = pl.pallas_call(
        local_kernel,
        grid=grid,
        in_specs=[
            cols(tokens), cols(tokens), cols(3, LEAD), filt_spec, cols(modes), cols(modes),
        ],
        out_specs=[cols(tokens), cols(block), cols(modes, pieces), cols(modes), cols(block)],
        out_shape=[
            jax.ShapeDtypeStruct((tokens, chans), bf16),
            jax.ShapeDtypeStruct((block, chans), f32),
            jax.ShapeDtypeStruct((modes, pieces, chans), f32),
            jax.ShapeDtypeStruct((modes, chans), f32),
            jax.ShapeDtypeStruct((block, chans), bf16),
        ],
        scratch_shapes=[
            pltpu.VMEM((LEAD + tokens, LANES), f32),
            pltpu.VMEM((LEAD + tokens, LANES), f32),
            pltpu.VMEM((tokens, LANES), f32),
        ],
        compiler_params=params,
        name="gate",
    )(k_in, v_in, lead, short_filter, residue, rate)

    peers = lax.axis_size("ctx")
    all_shape = (peers,) + state.shape
    y_part, all_states, before = pl.pallas_call(
        functools.partial(block_kernel, peers),
        grid=grid,
        in_specs=[
            cols(tokens), cols(block), cols(block), whole(fwd.shape), whole(rev.shape),
            whole(inv.shape), whole(state.shape), whole(tail.shape),
        ],
        out_specs=[cols(tokens), whole(all_shape), whole(tail.shape)],
        out_shape=[
            jax.ShapeDtypeStruct((tokens, chans), f32),
            jax.ShapeDtypeStruct(all_shape, f32),
            jax.ShapeDtypeStruct(tail.shape, bf16),
        ],
        scratch_shapes=[
            pltpu.VMEM(all_shape, f32),
            pltpu.VMEM(tail.shape, bf16),
            pltpu.SemaphoreType.DMA((peers,)),
            pltpu.SemaphoreType.DMA((peers,)),
            pltpu.SemaphoreType.DMA((2,)),
        ],
        compiler_params=pltpu.CompilerParams(
            collective_id=0, has_side_effects=True, vmem_limit_bytes=62 << 20
        ),
        name="block_conv",
    )(gated, h_rev, taps, fwd, rev, inv, state, tail)
    gap = lax.axis_index("ctx") - 1 - jnp.arange(all_states.shape[0])
    spans = (jnp.maximum(gap, 0) * tokens).astype(f32)[:, None, None]
    carried = jnp.where((gap >= 0)[:, None, None], jnp.exp(-rate[None] * spans) * all_states, 0.0)
    start = jnp.sum(carried, axis=0)

    product = pl.pallas_call(
        finish_kernel,
        grid=grid,
        in_specs=[
            cols(tokens), cols(modes, pieces), cols(modes), cols(block), cols(tokens),
            cols(3, LEAD), filt_spec, cols(block), cols(modes), cols(modes),
            whole(fwd.shape), whole(inv.shape),
        ],
        out_specs=cols(tokens),
        out_shape=jax.ShapeDtypeStruct((tokens, chans), bf16),
        scratch_shapes=[
            pltpu.VMEM((LEAD + tokens, LANES), f32),
            pltpu.VMEM((modes, block, LANES), f32),
            pltpu.VMEM((pieces, modes, LANES), f32),
        ],
        compiler_params=params,
        name="finish_conv",
    )(y_part, ends, start, before, q_in, lead, short_filter, taps, residue, rate, fwd, inv)

    return project(product, lax.all_gather(out_weight, "ctx", axis=1, tiled=True))


def solution(mesh):
    in_specs = (
        P("ctx", "mp"),
        P("ctx", "mp"),
        P("ctx", "mp"),
        P(None, None, "mp"),
        P(None, "mp"),
        P(None, "mp"),
        P(None, "mp"),
        P("mp", "ctx"),
    )
    out_specs = P("ctx", "mp")
    return jax.shard_map(local, mesh=mesh, in_specs=in_specs, out_specs=out_specs, check_vma=False)
```

```python
import functools

import jax
import jax.numpy as jnp
import numpy as np
from jax import lax
from jax.experimental import pallas as pl
from jax.experimental.pallas import tpu as pltpu
from jax.sharding import PartitionSpec as P

SHORT_LEN = 7
LANES = 128
LEAD = 8


def shifted(array, axis):
    peers = lax.axis_size(axis)
    return lax.ppermute(array, axis, [(i, i + 1) for i in range(peers - 1)])


def split_const(matrix):
    high = matrix.astype(jnp.bfloat16)
    low = (matrix - high.astype(np.float64)).astype(jnp.bfloat16)
    return jnp.asarray(np.stack([high, low]))


@functools.lru_cache
def dft_matrices(block):
    size = 2 * block
    freq = np.arange(block)[:, None]
    pos = np.arange(block)[None, :]
    angle = 2 * np.pi * ((freq * pos) % size) / size
    fwd = np.concatenate([np.cos(angle), -np.sin(angle)])
    fwd[block] = 1.0 - 2.0 * (np.arange(block) % 2)
    out_pos = block + np.arange(block)[:, None]
    freq = np.arange(block)[None, :]
    angle = 2 * np.pi * ((freq * out_pos) % size) / size
    real = 2 * np.cos(angle)
    imag = -2 * np.sin(angle)
    real[:, 0] = 1.0
    imag[:, 0] = 1.0 - 2.0 * (np.arange(block) % 2)
    inv = np.concatenate([real, imag], 1) / size
    return fwd, fwd[:, ::-1], inv


def mm(a, b):
    return jnp.dot(a, b, preferred_element_type=jnp.float32)


def mm_wide(pair, values):
    high = values.astype(jnp.bfloat16)
    low = (values - high.astype(jnp.float32)).astype(jnp.bfloat16)
    return mm(pair[0], high) + mm(pair[0], low) + mm(pair[1], high)


def spectrum_parts(spec, block, row0):
    real, imag = spec[:block], spec[block:]
    return real, jnp.where(row0, 0.0, imag), jnp.where(row0, imag, real)


def spectrum_mul(parts, spec, block):
    real, imag, cross = parts
    sr, si = spec[:block], spec[block:]
    return real * sr - imag * si, cross * si + imag * sr


def fill(scratch, lead_rows, signal):
    scratch[:LEAD] = lead_rows.astype(jnp.float32)
    scratch[LEAD:] = signal.astype(jnp.float32)


def short_taps(scratch, filt, start, block):
    total = filt[0:1] * scratch[LEAD + start : LEAD + start + block]
    for lag in range(1, SHORT_LEN):
        first = LEAD + start - lag
        total = total + filt[lag : lag + 1] * scratch[first : first + block]
    return total


def local_kernel(
    k_ref, v_ref, lead_ref, filt_ref, res_ref, rate_ref, gated_ref, h_rev_ref, ends_ref,
    state_ref, tail_ref, ks, vs, gs,
):
    block = h_rev_ref.shape[0]
    pieces = k_ref.shape[0] // block
    modes = rate_ref.shape[0]
    fill(ks, lead_ref[1], k_ref[...])
    fill(vs, lead_ref[2], v_ref[...])
    for b in range(pieces):
        gated = short_taps(ks, filt_ref[1], b * block, block) * short_taps(
            vs, filt_ref[2], b * block, block
        )
        rounded = gated.astype(jnp.bfloat16)
        gated_ref[b * block : (b + 1) * block] = rounded
        gs[b * block : (b + 1) * block] = rounded.astype(jnp.float32)
        if b == pieces - 1:
            tail_ref[...] = rounded
    rows = lax.broadcasted_iota(jnp.int32, (block, LANES), 0)
    back = (block - 1 - rows).astype(jnp.float32)

    def one_mode(n, h_rev):
        rate = rate_ref[pl.ds(n, 1), :]
        decay = jnp.exp(-rate * back)
        for b in range(pieces):
            ends_ref[n, b : b + 1, :] = jnp.sum(
                decay * gs[b * block : (b + 1) * block], axis=0, keepdims=True
            )
        return h_rev + (res_ref[pl.ds(n, 1), :] * jnp.sqrt(2.0 * rate)) * decay

    h_rev_ref[...] = lax.fori_loop(
        0, modes, one_mode, jnp.zeros((block, LANES), jnp.float32), unroll=2
    )

    step = jnp.exp(-rate_ref[...] * float(block))
    state = ends_ref[:, 0, :]
    for b in range(1, pieces):
        state = step * state + ends_ref[:, b, :]
    state_ref[...] = state


def block_kernel(
    peers, gated_ref, h_rev_ref, taps_ref, fwd_ref, rev_ref, inv_ref, states_ref, tail_ref,
    y_ref, all_ref, before_ref, landed, landed_tail, send, recv, tail_sems,
):
    index = pl.program_id(0)

    @pl.when(index == 0)
    def _():
        exchange_start(peers, states_ref, tail_ref, landed, landed_tail, send, recv, tail_sems)

    block = taps_ref.shape[0]
    pieces = gated_ref.shape[0] // block
    rows = lax.broadcasted_iota(jnp.int32, (block, LANES), 0)
    row0 = rows == 0
    sign = (1 - 2 * (rows % 2)).astype(jnp.float32)
    sign = jnp.concatenate([sign, sign], 0)
    taps_spec = mm_wide(fwd_ref, taps_ref[...])
    near_spec = sign * (taps_spec + mm_wide(rev_ref, h_rev_ref[...]))
    far = spectrum_parts(taps_spec, block, row0)
    near = spectrum_parts(near_spec, block, row0)
    previous = None
    for b in range(pieces):
        signal = gated_ref[b * block : (b + 1) * block]
        spec = mm(fwd_ref[0], signal) + mm(fwd_ref[1], signal)
        real, imag = spectrum_mul(near, spec, block)
        if previous is not None:
            more_real, more_imag = spectrum_mul(far, previous, block)
            real, imag = real + more_real, imag + more_imag
        y_ref[b * block : (b + 1) * block] = mm_wide(inv_ref, jnp.concatenate([real, imag], 0))
        previous = spec

    @pl.when(index == pl.num_programs(0) - 1)
    def _():
        exchange_finish(peers, states_ref, tail_ref, landed, landed_tail, send, recv, tail_sems)
        all_ref[...] = landed[...]
        before_ref[...] = landed_tail[...]


def finish_kernel(
    y_ref, ends_ref, start_ref, tail_ref, q_ref, lead_ref, filt_ref, taps_ref, res_ref, rate_ref,
    fwd_ref, inv_ref, out_ref, qs, lift, states,
):
    block = taps_ref.shape[0]
    pieces = q_ref.shape[0] // block
    modes = rate_ref.shape[0]
    fill(qs, lead_ref[0], q_ref[...])
    rows = lax.broadcasted_iota(jnp.int32, (block, LANES), 0)
    ahead = (rows + 1).astype(jnp.float32)
    for n in range(modes):
        rate = rate_ref[n : n + 1, :]
        lift[n] = (res_ref[n : n + 1, :] * jnp.sqrt(2.0 * rate)) * jnp.exp(-rate * ahead)
    step = jnp.exp(-rate_ref[...] * float(block))
    state = start_ref[...]
    states[0] = state
    for b in range(1, pieces):
        state = step * state + ends_ref[:, b - 1, :]
        states[b] = state
    taps_spec = mm_wide(fwd_ref, taps_ref[...])
    far = spectrum_parts(taps_spec, block, rows == 0)
    tail = tail_ref[...]
    spec = mm(fwd_ref[0], tail) + mm(fwd_ref[1], tail)
    halo = mm_wide(inv_ref, jnp.concatenate(spectrum_mul(far, spec, block), 0))
    for b in range(pieces):
        span = slice(b * block, (b + 1) * block)
        total = y_ref[span]
        if b == 0:
            total = total + halo
        for n in range(modes):
            total = total + lift[n] * states[b, n : n + 1, :]
        q_short = short_taps(qs, filt_ref[0], b * block, block).astype(jnp.bfloat16)
        long_conv = total.astype(jnp.bfloat16)
        out_ref[span] = (q_short.astype(jnp.float32) * long_conv.astype(jnp.float32)).astype(
            jnp.bfloat16
        )

MESH = pl.DeviceIdType.MESH


def tail_copy(peer, tail_ref, before_ref, tail_sems):
    return pltpu.make_async_remote_copy(
        src_ref=tail_ref, dst_ref=before_ref, send_sem=tail_sems.at[0],
        recv_sem=tail_sems.at[1], device_id={"ctx": peer}, device_id_type=MESH,
    )


def state_copy(peer, slot, hop, state_ref, all_ref, send, recv):
    return pltpu.make_async_remote_copy(
        src_ref=state_ref, dst_ref=all_ref.at[slot], send_sem=send.at[hop],
        recv_sem=recv.at[slot], device_id={"ctx": peer}, device_id_type=MESH,
    )


def exchange_start(peers, state_ref, tail_ref, all_ref, before_ref, send, recv, tail_sems):
    me = lax.axis_index("ctx")
    barrier = pltpu.get_barrier_semaphore()
    for hop in range(1, peers):
        pl.semaphore_signal(
            barrier, inc=1, device_id={"ctx": lax.rem(me + hop, peers)}, device_id_type=MESH
        )
    pl.semaphore_wait(barrier, peers - 1)

    @pl.when(me < peers - 1)
    def _():
        tail_copy(me + 1, tail_ref, before_ref, tail_sems).start()

    for hop in range(1, peers):
        state_copy(lax.rem(me + hop, peers), me, hop, state_ref, all_ref, send, recv).start()
    all_ref[me] = state_ref[...]

    @pl.when(me == 0)
    def _():
        before_ref[...] = jnp.zeros_like(before_ref)


def exchange_finish(peers, state_ref, tail_ref, all_ref, before_ref, send, recv, tail_sems):
    me = lax.axis_index("ctx")
    for hop in range(1, peers):
        source = lax.rem(me + hop, peers)
        state_copy(source, source, hop, state_ref, all_ref, send, recv).wait_recv()
        state_copy(source, me, hop, state_ref, all_ref, send, recv).wait_send()

    @pl.when(me > 0)
    def _():
        tail_copy(me, tail_ref, before_ref, tail_sems).wait_recv()

    @pl.when(me < peers - 1)
    def _():
        tail_copy(me + 1, tail_ref, before_ref, tail_sems).wait_send()


def project_kernel(
    prod_ref, w_ref, out_ref, near_out, near_in, far_out, far_in, mine_out, mine_in, hold, total,
    sems,
):
    me = lax.axis_index("mp")
    high, low = me // 2, lax.rem(me, 2)
    pair = high * 2 + (1 - low)
    across = (1 - high) * 2 + low
    chunks, rows, width = near_out.shape
    step = 256

    barrier = pltpu.get_barrier_semaphore()
    for peer in (pair, across):
        pl.semaphore_signal(barrier, inc=1, device_id={"mp": peer}, device_id_type=MESH)
    pl.semaphore_wait(barrier, 2)

    def copy(kind, t, source, target, peer):
        return pltpu.make_async_remote_copy(
            src_ref=source.at[t], dst_ref=target.at[t], send_sem=sems.at[2 * kind, t],
            recv_sem=sems.at[2 * kind + 1, t], device_id={"mp": peer}, device_id_type=MESH,
        )

    def near_copy(t):
        return copy(0, t, near_out, near_in, pair)

    def far_copy(t):
        return copy(1, t, far_out, far_in, across)

    def mine_copy(t):
        return copy(2, t, mine_out, mine_in, pair)

    def partial(t, owner, put):
        left = prod_ref[pl.ds(pl.multiple_of(t * rows, rows), rows), :]
        for col in range(0, width, step):
            first = pl.multiple_of(owner * width + col, step)
            put(col, mm(left, w_ref[:, pl.ds(first, step)]))

    def send_near(t):
        def put(col, value):
            near_out[t, :, col : col + step] = value.astype(jnp.bfloat16)

        partial(t, (1 - high) * 2 + (1 - low), put)
        near_copy(t).start()

        def keep(col, value):
            hold[t, :, col : col + step] = value

        partial(t, across, keep)

    def send_far(t):
        near_copy(t).wait_recv()
        far_out[t] = (hold[t] + near_in[t].astype(jnp.float32)).astype(jnp.bfloat16)
        far_copy(t).start()

    def first_pass(t, carry):
        send_near(t)

        @pl.when(t > 0)
        def _():
            send_far(t - 1)

        return carry

    lax.fori_loop(0, chunks, first_pass, 0)
    send_far(chunks - 1)

    def second_pass(t, carry):
        def put(col, value):
            mine_out[t, :, col : col + step] = value.astype(jnp.bfloat16)

        partial(t, pair, put)
        mine_copy(t).start()

        def keep(col, value):
            total[t, :, col : col + step] = value

        partial(t, me, keep)
        return carry

    lax.fori_loop(0, chunks, second_pass, 0)

    def finish(t, carry):
        mine_copy(t).wait_recv()
        far_copy(t).wait_recv()
        summed = total[t] + mine_in[t].astype(jnp.float32) + far_in[t].astype(jnp.float32)
        out_ref[pl.ds(pl.multiple_of(t * rows, rows), rows), :] = summed.astype(jnp.bfloat16)
        near_copy(t).wait_send()
        far_copy(t).wait_send()
        mine_copy(t).wait_send()
        return carry

    lax.fori_loop(0, chunks, finish, 0)


def project(product, weight):
    tokens = product.shape[0]
    width = weight.shape[1] // lax.axis_size("mp")
    chunks = 8
    box = (chunks, tokens // chunks, width)
    vmem = pl.BlockSpec(memory_space=pltpu.VMEM)
    return pl.pallas_call(
        project_kernel,
        in_specs=[vmem] * 2,
        out_specs=vmem,
        out_shape=jax.ShapeDtypeStruct((tokens, width), jnp.bfloat16),
        scratch_shapes=[pltpu.VMEM(box, jnp.bfloat16)] * 6
        + [pltpu.VMEM(box, jnp.float32)] * 2
        + [pltpu.SemaphoreType.DMA((6, chunks))],
        compiler_params=pltpu.CompilerParams(
            collective_id=1, has_side_effects=True, vmem_limit_bytes=48 << 20
        ),
        name="project",
    )(product, weight)


def ring_place(chip, count):
    odd = chip % 2
    return (chip // 2) * (1 - odd) + (count - 1 - chip // 2) * odd


def ring_chip(place, count):
    back = place // (count // 2)
    return 2 * place * (1 - back) + (2 * (count - 1 - place) + 1) * back


LEAD_ROWS = 16
CHUNKS = 4


def spread(rows):
    return jnp.stack([jnp.broadcast_to(rows[n : n + 1], (8, LANES)) for n in range(rows.shape[0])])


def packed_product(near, spec, far, previous):
    block = spec.shape[0] // 2
    nr, ni, sr, si = near[:block], near[block:], spec[:block], spec[block:]
    fr, fi, pr, pi = far[:block], far[block:], previous[:block], previous[block:]
    real = (nr * sr - ni * si) + (fr * pr - fi * pi)
    imag = (nr * si + ni * sr) + (fr * pi + fi * pr)
    row0 = lax.broadcasted_iota(jnp.int32, (8, LANES), 0) == 0
    real_top = jnp.where(row0, nr[:8] * sr[:8] + fr[:8] * pr[:8], real[:8])
    imag_top = jnp.where(row0, ni[:8] * si[:8] + fi[:8] * pi[:8], imag[:8])
    return jnp.concatenate([real_top, real[8:], imag_top, imag[8:]], 0)


def fused_kernel(
    peers, q_ref, k_ref, v_ref, w_ref, filt_ref, taps_ref, res_ref, rate_ref, fwd3_ref, fwd2_ref,
    inv_ref, out_ref, qbuf, kbuf, vbuf, ks, vs, gbuf, before, hold, ends_ref, state_ref, peer_ref,
    prefix_ref, onward_ref, start_ref, near_ref, far_ref, y_ref, prod_ref, ring, part, pair_in,
    cross_out, cross_in, load_sems, own_sems, halo_sems, tail_sems, state_sems, ring_sems,
    pair_sems, cross_sems,
):
    tokens, chans = prod_ref.shape
    block = taps_ref.shape[0]
    pieces = tokens // block
    modes = rate_ref.shape[0]
    blocks = chans // LANES
    f32, bf16 = jnp.float32, jnp.bfloat16
    ctx = lax.axis_index("ctx")
    me = lax.axis_index("mp")
    high, low = me // 2, lax.rem(me, 2)
    pair = high * 2 + (1 - low)
    across = (1 - high) * 2 + low
    place = ring_place(ctx, peers)

    def neighbour(offset):
        return ring_chip(lax.rem(place + offset + peers, peers), peers)

    ahead, behind = neighbour(1), neighbour(-1)

    loads = [
        pltpu.make_async_copy(src, dst.at[pl.ds(LEAD_ROWS, tokens)], load_sems.at[n])
        for n, (src, dst) in enumerate(((k_ref, kbuf), (v_ref, vbuf), (q_ref, qbuf)))
    ]
    owns = [
        pltpu.make_async_copy(
            w_ref.at[:, pl.ds(k * LANES, LANES)], ring.at[ctx, k], own_sems.at[k]
        )
        for k in range(CHUNKS)
    ]
    for copy in owns + loads:
        copy.start()

    barrier = pltpu.get_barrier_semaphore()
    for hop in range(1, peers):
        pl.semaphore_signal(
            barrier, inc=1, device_id={"ctx": lax.rem(ctx + hop, peers)}, device_id_type=MESH
        )
    for peer in (pair, across):
        pl.semaphore_signal(barrier, inc=1, device_id={"mp": peer}, device_id_type=MESH)
    pl.semaphore_wait(barrier, peers + 1)

    def halo_copy(n, src, dst, peer):
        return pltpu.make_async_remote_copy(
            src_ref=src.at[pl.ds(tokens - LEAD_ROWS, LEAD_ROWS)], dst_ref=dst.at[pl.ds(0, LEAD_ROWS)],
            send_sem=halo_sems.at[0, n], recv_sem=halo_sems.at[1, n],
            device_id={"ctx": peer}, device_id_type=MESH,
        )

    halos = ((k_ref, kbuf), (v_ref, vbuf), (q_ref, qbuf))

    @pl.when(ctx < peers - 1)
    def _():
        for n, (src, dst) in enumerate(halos):
            halo_copy(n, src, dst, ctx + 1).start()

    def ring_copy(way, seq, chip, k):
        return pltpu.make_async_remote_copy(
            src_ref=ring.at[chip, k], dst_ref=ring.at[chip, k],
            send_sem=ring_sems.at[2 * way, seq], recv_sem=ring_sems.at[2 * way + 1, seq],
            device_id={"ctx": behind if way else ahead}, device_id_type=MESH,
        )

    def send_own(k):
        for way in (0, 1):
            ring_copy(way, k, ctx, k).start()

    for copy in owns:
        copy.wait()
    send_own(0)
    send_own(1)

    def chunk_at(seq, way):
        hop = seq // CHUNKS
        chip = neighbour(hop + 1 if way else -hop - 1)
        return chip, seq % CHUNKS + 2 * way * (hop // 3)

    def arrive(seq):
        for way in (0, 1):
            chip, k = chunk_at(seq, way)
            ring_copy(way, seq, chip, k).wait_recv()

            @pl.when(seq < 8 + 2 * (1 - way))
            def _():
                ring_copy(way, seq + CHUNKS, chip, k).start()

            if way:
                @pl.when((seq >= 10) & (seq < 12))
                def _():
                    ring_copy(way, seq + 2, chip, k).start()

    @pl.when(ctx == 0)
    def _():
        for _, dst in halos:
            dst[0:LEAD_ROWS] = jnp.zeros((LEAD_ROWS, chans), bf16)
        before[...] = jnp.zeros_like(before)

    def halo_wait(n):
        @pl.when(ctx > 0)
        def _():
            halo_copy(n, *halos[n], ctx).wait_recv()

    def lanes(i):
        return pl.ds(pl.multiple_of(i * LANES, LANES), LANES)

    def short(scratch, branch, b, col):
        first = LEAD_ROWS + b * block
        total = filt_ref[branch, 0:1, col] * scratch[first : first + block]
        for lag in range(1, SHORT_LEN):
            total = total + filt_ref[branch, lag : lag + 1, col] * scratch[
                first - lag : first - lag + block
            ]
        return total

    sub = lax.broadcasted_iota(jnp.int32, (8, LANES), 0).astype(f32)

    for n in (0, 1):
        loads[n].wait()
        halo_wait(n)

    row, side_y = ctx // 2, lax.rem(ctx, 2)
    partner = ctx + 1 - 2 * side_y

    halves = 2
    part_blocks = blocks // halves

    def half(h):
        width = chans // halves
        return pl.ds(pl.multiple_of(h * width, width), width)

    def tail_copy(peer):
        return pltpu.make_async_remote_copy(
            src_ref=gbuf.at[pl.ds(tokens - block, block)], dst_ref=before, send_sem=tail_sems.at[0], recv_sem=tail_sems.at[1],
            device_id={"ctx": peer}, device_id_type=MESH,
        )

    def state_copy(h):
        return pltpu.make_async_remote_copy(
            src_ref=state_ref.at[:, half(h)], dst_ref=peer_ref.at[:, half(h)],
            send_sem=state_sems.at[0, h], recv_sem=state_sems.at[1, h],
            device_id={"ctx": partner}, device_id_type=MESH,
        )

    def prefix_copy(peer, h):
        return pltpu.make_async_remote_copy(
            src_ref=onward_ref.at[:, half(h)], dst_ref=prefix_ref.at[:, half(h)],
            send_sem=state_sems.at[2, h], recv_sem=state_sems.at[3, h],
            device_id={"ctx": peer}, device_id_type=MESH,
        )

    def gate_body(i, carry):
        col = lanes(i)
        ks[...] = kbuf[:, col].astype(f32)
        vs[...] = vbuf[:, col].astype(f32)
        rate = rate_ref[:, col]
        d8 = spread(jnp.exp(-8.0 * rate))
        last = jnp.exp(-spread(rate) * (7.0 - sub)[None])
        acc = jnp.zeros((modes, 8, LANES), f32)
        for b in range(pieces):
            gated = short(ks, 1, b, col) * short(vs, 2, b, col)
            rounded = gated.astype(bf16)
            gbuf[b * block : (b + 1) * block, col] = rounded
            back = rounded.astype(f32)
            for r in range(block // 8):
                acc = acc * d8 + back[8 * r : 8 * r + 8][None]
            hold[b] = (acc * last).reshape(modes * 8, LANES)
        for b in range(pieces):
            ends = hold[b, pl.ds(0, modes, stride=8), :]
            for j in range(1, 8):
                ends = ends + hold[b, pl.ds(j, modes, stride=8), :]
            ends_ref[b, :, col] = ends
            if b == pieces - 1:
                state_ref[:, col] = ends

        @pl.when(lax.rem(i, part_blocks) == part_blocks - 1)
        def _():
            state_copy(i // part_blocks).start()

        @pl.when(i == blocks - 2)
        def _():
            send_own(2)

        return carry

    lax.fori_loop(0, blocks, gate_body, 0)

    def chain(j):
        col = half(j)
        state_copy(j).wait_recv()
        decay = jnp.exp(-rate_ref[:, col] * float(tokens))
        mine, other = state_ref[:, col], peer_ref[:, col]
        first = jnp.where(side_y == 0, mine, other)
        second = jnp.where(side_y == 0, other, mine)

        @pl.when(row > 0)
        def _():
            prefix_copy(ctx, j).wait_recv()

        @pl.when(row == 0)
        def _():
            prefix_ref[:, col] = jnp.zeros((modes, chans // halves), f32)

        prefix = prefix_ref[:, col]
        between = prefix * decay + first

        @pl.when(row < peers // 2 - 1)
        def _():
            onward_ref[:, col] = between * decay + second
            prefix_copy(ctx + 2, j).start()

        start_ref[:, col] = jnp.where(side_y == 0, prefix, between)

    def chain_at(place_in_order):
        h = place_in_order - row

        @pl.when((h >= 0) & (h < halves))
        def _():
            chain(h)

        @pl.when((h == halves - 1) & (row < peers // 2 - 1))
        def _():
            tail_copy(ctx + 1).start()

    chain_at(0)

    sign = (1 - 2 * (lax.broadcasted_iota(jnp.int32, (2 * block, LANES), 0) % 2)).astype(f32)

    def spectrum(*signals):
        both = jnp.concatenate(signals, 1)
        return mm(fwd2_ref[...], jnp.concatenate([both, both], 0))

    def conv_body(i, carry):
        col = lanes(i)
        rate = rate_ref[:, col]
        d8 = spread(jnp.exp(-8.0 * rate))
        u = spread(res_ref[:, col] * jnp.sqrt(2.0 * rate)) * jnp.exp(-spread(rate) * sub[None])
        rows = []
        for r in range(block // 8):
            rows.append(jnp.sum(u, axis=0))
            if r < block // 8 - 1:
                u = u * d8
        taps = taps_ref[:, col]
        values = jnp.concatenate([taps, taps + jnp.concatenate(rows, 0)], 1)
        top = values.astype(bf16)
        rest = (values - top.astype(f32)).astype(bf16)
        filters = mm(fwd3_ref[...], jnp.concatenate([top, rest, top], 0))
        far_ref[:, col] = filters[:, :LANES]
        near_ref[:, col] = sign * filters[:, LANES:]
        previous = None
        waiting = []
        for b in range(0, pieces, 2):
            both = spectrum(
                gbuf[b * block : (b + 1) * block, col], gbuf[(b + 1) * block : (b + 2) * block, col]
            )
            for half in (0, 1):
                spec = both[:, half * LANES : (half + 1) * LANES]
                if previous is not None:
                    waiting.append(
                        packed_product(near_ref[:, col], spec, far_ref[:, col], previous).astype(bf16)
                    )
                previous = spec
                done = b + half
                if len(waiting) == 2 or (waiting and done == pieces - 1):
                    count = len(waiting)
                    y = mm(inv_ref[...], jnp.concatenate(waiting, 1))
                    for n in range(count):
                        at = (done - count + 1 + n) * block
                        y_ref[at : at + block, col] = y[:, n * LANES : (n + 1) * LANES]
                    waiting = []

        @pl.when(i == 1)
        def _():
            send_own(3)

        @pl.when(i == blocks - 1)
        def _():
            arrive(0)

        @pl.when((i == 2) & (ctx == peers - 2))
        def _():
            tail_copy(ctx + 1).start()

        for n in (1, 2):
            @pl.when(i == 3 * n - 1)
            def _():
                chain_at(n)

        return carry

    lax.fori_loop(0, blocks, conv_body, 0)

    chain_at(3)

    loads[2].wait()
    halo_wait(2)

    def finish_piece(b, near, state, lift, d8, col):
        u = lift * spread(state)
        rows = []
        for r in range(block // 8):
            rows.append(jnp.sum(u, axis=0))
            if r < block // 8 - 1:
                u = u * d8
        long_conv = (near + jnp.concatenate(rows, 0)).astype(bf16)
        q_short = short(ks, 0, b, col).astype(bf16)
        prod_ref[b * block : (b + 1) * block, col] = (
            q_short.astype(f32) * long_conv.astype(f32)
        ).astype(bf16)

    def lifts(col):
        rate = rate_ref[:, col]
        lift = spread(res_ref[:, col] * jnp.sqrt(2.0 * rate)) * jnp.exp(
            -spread(rate) * (sub + 1.0)[None]
        )
        return lift, spread(jnp.exp(-8.0 * rate))

    def finish_body(i, carry):
        col = lanes(i)

        @pl.when(i == part_blocks)
        def _():
            chain_at(4)
            arrive(1)

        ks[...] = qbuf[:, col].astype(f32)
        lift, d8 = lifts(col)
        step = jnp.exp(-rate_ref[:, col] * float(block))
        base = start_ref[:, col]
        for b in range(1, pieces):
            base = base * step
            near = y_ref[b * block : (b + 1) * block, col]
            finish_piece(b, near, base + ends_ref[b - 1, :, col], lift, d8, col)
        return carry

    lax.fori_loop(0, blocks, finish_body, 0)

    @pl.when(ctx > 0)
    def _():
        tail_copy(ctx).wait_recv()

    def first_body(i, carry):
        col = lanes(i)
        first = LEAD_ROWS + block
        ks[:first] = qbuf[:first, col].astype(f32)
        both = spectrum(before[:, col], gbuf[0:block, col])
        spec = packed_product(
            near_ref[:, col], both[:, LANES:], far_ref[:, col], both[:, :LANES]
        ).astype(bf16)
        lift, d8 = lifts(col)
        finish_piece(0, mm(inv_ref[...], spec), start_ref[:, col], lift, d8, col)
        return carry

    lax.fori_loop(0, blocks, first_body, 0)

    arrive(2)
    arrive(3)

    events = 2 + 3 * CHUNKS + CHUNKS // 2
    row_step = 256
    strips = tokens // row_step

    def chunk_of(t, side):
        own = 1 - (t + 14) // 16
        seq = (t - 2) * (1 - own)
        chip, k = chunk_at(seq, side)
        return own * ctx + (1 - own) * chip, own * (2 * t + side) + (1 - own) * k

    def role(chip, k):
        owner = chip // 2
        gap = owner // 2 - high
        cross = gap * gap
        sub_slot = lax.rem(chip, 2) * CHUNKS + k
        return lax.rem(owner, 2) == low, cross, (owner // 2) * 2 * CHUNKS + sub_slot, sub_slot

    def pair_copy(chip, k, slot, r):
        at = pl.ds(pl.multiple_of(r * row_step, row_step), row_step)
        return pltpu.make_async_remote_copy(
            src_ref=part.at[chip, k, at], dst_ref=pair_in.at[slot, at],
            send_sem=pair_sems.at[0, slot * strips + r], recv_sem=pair_sems.at[1, slot * strips + r],
            device_id={"mp": pair}, device_id_type=MESH,
        )

    def cross_copy(slot, r):
        at = pl.ds(pl.multiple_of(r * row_step, row_step), row_step)
        return pltpu.make_async_remote_copy(
            src_ref=cross_out.at[slot, at], dst_ref=cross_in.at[slot, at],
            send_sem=cross_sems.at[0, slot * strips + r],
            recv_sem=cross_sems.at[1, slot * strips + r],
            device_id={"mp": across}, device_id_type=MESH,
        )

    def settle(spots, roles, r):
        at = pl.ds(pl.multiple_of(r * row_step, row_step), row_step)
        for (chip, k), (mine, cross, slot, sub_slot) in zip(spots, roles):
            @pl.when(mine & (cross == 1))
            def _():
                pair_copy(chip, k, slot, r).wait_recv()
                total = part[chip, k, at, :].astype(f32) + pair_in[slot, at, :].astype(f32)
                cross_out[sub_slot, at, :] = total.astype(bf16)
                cross_copy(sub_slot, r).start()

    def total(n):
        slot = high * 2 * CHUNKS + n
        chip, k = 2 * me + n // CHUNKS, n % CHUNKS
        for r in range(strips):
            pair_copy(chip, k, slot, r).wait_recv()
            cross_copy(n, r).wait_recv()
        value = part[chip, k].astype(f32) + pair_in[slot].astype(f32) + cross_in[n].astype(f32)
        out_ref[:, n * LANES : (n + 1) * LANES] = value.astype(bf16)

    def time_of(chip, n):
        gap = lax.rem(ring_place(chip, peers) - place + peers, peers)
        own, far = 1 - (gap + peers - 1) // peers, gap // (peers // 2)
        hop = (1 - far) * (gap - 1) + far * (peers - 1 - gap)
        k = n % CHUNKS
        return own * (k // 2) + (1 - own) * (2 + CHUNKS * hop + k - 2 * (hop // 3) * (k // 2))

    def event(t, carry):
        for n in range(3):
            @pl.when(t == 2 * n)
            def _():
                arrive(CHUNKS + n)

        @pl.when(t >= 5 + CHUNKS)
        def _():
            arrive(t - 2)

        spots = [chunk_of(t, side) for side in (0, 1)]
        roles = [role(*spot) for spot in spots]

        def products(r, carry):
            at = pl.ds(pl.multiple_of(r * row_step, row_step), row_step)
            right = jnp.concatenate([ring[chip, k] for chip, k in spots], 1)
            value = mm(prod_ref[at, :], right).astype(bf16)
            for n, ((chip, k), (mine, _, slot, _)) in enumerate(zip(spots, roles)):
                part[chip, k, at, :] = value[:, n * LANES : (n + 1) * LANES]

                @pl.when(jnp.logical_not(mine))
                def _():
                    pair_copy(chip, k, slot, r).start()

            @pl.when(r > 0)
            def _():
                settle(spots, roles, r - 1)

            return carry

        lax.fori_loop(0, strips, products, 0)
        settle(spots, roles, strips - 1)
        return carry

    early = events - 4
    lax.fori_loop(0, events - 1, event, 0)
    for n in range(2 * CHUNKS):
        @pl.when(time_of(2 * me + n // CHUNKS, n) <= early)
        def _():
            total(n)

    def sent_at(n):
        chip = 4 * (n // (2 * CHUNKS)) + 2 * (1 - low) + n % (2 * CHUNKS) // CHUNKS
        return time_of(chip, n)

    def pair_sent(n):
        for r in range(strips):
            pair_copy(0, 0, n, r).wait_send()

    for n in range(4 * CHUNKS):
        @pl.when(sent_at(n) <= early)
        def _():
            pair_sent(n)

    for way in (0, 1):
        for seq in range(3 * CHUNKS):
            ring_copy(way, seq, ctx, 0).wait_send()

    @pl.when(ctx < peers - 1)
    def _():
        for n, (src, dst) in enumerate(halos):
            halo_copy(n, src, dst, ctx + 1).wait_send()
        tail_copy(ctx + 1).wait_send()

    for j in range(halves):
        state_copy(j).wait_send()

    @pl.when(row < peers // 2 - 1)
    def _():
        for j in range(halves):
            prefix_copy(ctx + 2, j).wait_send()

    lax.fori_loop(events - 1, events, event, 0)
    for n in range(2 * CHUNKS):
        @pl.when(time_of(2 * me + n // CHUNKS, n) > early)
        def _():
            total(n)

    for n in range(4 * CHUNKS):
        @pl.when(sent_at(n) > early)
        def _():
            pair_sent(n)

    for n in range(2 * CHUNKS):
        for r in range(strips):
            cross_copy(n, r).wait_send()
    for way in (0, 1):
        for seq in range(3 * CHUNKS, 3 * CHUNKS + CHUNKS // 2):
            ring_copy(way, seq, ctx, 0).wait_send()


def fused(q_in, k_in, v_in, short_filter, taps, residue, rate, out_weight):
    tokens, chans = q_in.shape
    block = taps.shape[0]
    modes = rate.shape[0]
    pieces = tokens // block
    peers = lax.axis_size("ctx")
    f32, bf16 = jnp.float32, jnp.bfloat16
    fwd, _, inv = dft_matrices(block)
    high = fwd.astype(jnp.bfloat16)
    low = (fwd - high.astype(np.float64)).astype(jnp.bfloat16)
    fwd3 = jnp.asarray(np.concatenate([high, high, low], 1))
    fwd2 = jnp.asarray(np.concatenate([high, low], 1))
    inv1 = jnp.asarray(inv.astype(jnp.bfloat16))
    vmem = pl.BlockSpec(memory_space=pltpu.VMEM)
    hbm = pl.BlockSpec(memory_space=pl.ANY)
    padded = (LEAD_ROWS + tokens, chans)
    narrow = (LEAD_ROWS + tokens, LANES)
    dma = pltpu.SemaphoreType.DMA
    return pl.pallas_call(
        functools.partial(fused_kernel, peers),
        in_specs=[hbm] * 4 + [vmem] * 7,
        out_specs=vmem,
        out_shape=jax.ShapeDtypeStruct((tokens, chans), bf16),
        scratch_shapes=[pltpu.VMEM(padded, bf16)] * 3
        + [pltpu.VMEM(narrow, f32)] * 2
        + [
            pltpu.VMEM((tokens, chans), bf16),
            pltpu.VMEM((block, chans), bf16),
            pltpu.VMEM((pieces, modes * 8, LANES), f32),
            pltpu.VMEM((pieces, modes, chans), f32),
            pltpu.VMEM((modes, chans), f32),
            pltpu.VMEM((modes, chans), f32),
            pltpu.VMEM((modes, chans), f32),
            pltpu.VMEM((modes, chans), f32),
            pltpu.VMEM((modes, chans), f32),
            pltpu.VMEM((2 * block, chans), f32),
            pltpu.VMEM((2 * block, chans), f32),
            pltpu.VMEM((tokens, chans), f32),
            pltpu.VMEM((tokens, chans), bf16),
            pltpu.VMEM((peers, CHUNKS, chans, LANES), bf16),
            pltpu.VMEM((peers, CHUNKS, tokens, LANES), bf16),
            pltpu.VMEM((4 * CHUNKS, tokens, LANES), bf16),
            pltpu.VMEM((2 * CHUNKS, tokens, LANES), bf16),
            pltpu.VMEM((2 * CHUNKS, tokens, LANES), bf16),
            dma((3,)), dma((CHUNKS,)), dma((2, 3)), dma((2,)), dma((4, 2)),
            dma((4, 4 * CHUNKS)),
            dma((2, 4 * CHUNKS * (tokens // 256))), dma((2, 2 * CHUNKS * (tokens // 256))),
        ],
        compiler_params=pltpu.CompilerParams(
            collective_id=2, has_side_effects=True, vmem_limit_bytes=60 << 20
        ),
        name="fused",
    )(q_in, k_in, v_in, out_weight, short_filter, taps, residue, rate, fwd3, fwd2, inv1)


def cols(*lead):
    return pl.BlockSpec(lead + (LANES,), lambda i: (0,) * len(lead) + (i,))


def whole(shape):
    return pl.BlockSpec(shape, lambda i: (0,) * len(shape))


def local(q_in, k_in, v_in, short_filter, taps, residue, rate, out_weight):
    tokens, chans = q_in.shape
    block = taps.shape[0]
    modes = rate.shape[0]
    pieces = tokens // block
    columns = out_weight.shape[1]
    if (lax.axis_size("ctx"), lax.axis_size("mp"), columns) == (8, 4, CHUNKS * LANES):
        return fused(q_in, k_in, v_in, short_filter, taps, residue, rate, out_weight)
    fwd, rev, inv = [split_const(m) for m in dft_matrices(block)]
    grid = (chans // LANES,)
    f32, bf16 = jnp.float32, jnp.bfloat16
    lead = shifted(jnp.stack([q_in[-LEAD:], k_in[-LEAD:], v_in[-LEAD:]]), "ctx")
    filt_spec = cols(3, SHORT_LEN)
    params = pltpu.CompilerParams(vmem_limit_bytes=62 << 20)
    gated, h_rev, ends, state, tail = pl.pallas_call(
        local_kernel,
        grid=grid,
        in_specs=[
            cols(tokens), cols(tokens), cols(3, LEAD), filt_spec, cols(modes), cols(modes),
        ],
        out_specs=[cols(tokens), cols(block), cols(modes, pieces), cols(modes), cols(block)],
        out_shape=[
            jax.ShapeDtypeStruct((tokens, chans), bf16),
            jax.ShapeDtypeStruct((block, chans), f32),
            jax.ShapeDtypeStruct((modes, pieces, chans), f32),
            jax.ShapeDtypeStruct((modes, chans), f32),
            jax.ShapeDtypeStruct((block, chans), bf16),
        ],
        scratch_shapes=[
            pltpu.VMEM((LEAD + tokens, LANES), f32),
            pltpu.VMEM((LEAD + tokens, LANES), f32),
            pltpu.VMEM((tokens, LANES), f32),
        ],
        compiler_params=params,
        name="gate",
    )(k_in, v_in, lead, short_filter, residue, rate)

    peers = lax.axis_size("ctx")
    all_shape = (peers,) + state.shape
    y_part, all_states, before = pl.pallas_call(
        functools.partial(block_kernel, peers),
        grid=grid,
        in_specs=[
            cols(tokens), cols(block), cols(block), whole(fwd.shape), whole(rev.shape),
            whole(inv.shape), whole(state.shape), whole(tail.shape),
        ],
        out_specs=[cols(tokens), whole(all_shape), whole(tail.shape)],
        out_shape=[
            jax.ShapeDtypeStruct((tokens, chans), f32),
            jax.ShapeDtypeStruct(all_shape, f32),
            jax.ShapeDtypeStruct(tail.shape, bf16),
        ],
        scratch_shapes=[
            pltpu.VMEM(all_shape, f32),
            pltpu.VMEM(tail.shape, bf16),
            pltpu.SemaphoreType.DMA((peers,)),
            pltpu.SemaphoreType.DMA((peers,)),
            pltpu.SemaphoreType.DMA((2,)),
        ],
        compiler_params=pltpu.CompilerParams(
            collective_id=0, has_side_effects=True, vmem_limit_bytes=62 << 20
        ),
        name="block_conv",
    )(gated, h_rev, taps, fwd, rev, inv, state, tail)
    gap = lax.axis_index("ctx") - 1 - jnp.arange(all_states.shape[0])
    spans = (jnp.maximum(gap, 0) * tokens).astype(f32)[:, None, None]
    carried = jnp.where((gap >= 0)[:, None, None], jnp.exp(-rate[None] * spans) * all_states, 0.0)
    start = jnp.sum(carried, axis=0)

    product = pl.pallas_call(
        finish_kernel,
        grid=grid,
        in_specs=[
            cols(tokens), cols(modes, pieces), cols(modes), cols(block), cols(tokens),
            cols(3, LEAD), filt_spec, cols(block), cols(modes), cols(modes),
            whole(fwd.shape), whole(inv.shape),
        ],
        out_specs=cols(tokens),
        out_shape=jax.ShapeDtypeStruct((tokens, chans), bf16),
        scratch_shapes=[
            pltpu.VMEM((LEAD + tokens, LANES), f32),
            pltpu.VMEM((modes, block, LANES), f32),
            pltpu.VMEM((pieces, modes, LANES), f32),
        ],
        compiler_params=params,
        name="finish_conv",
    )(y_part, ends, start, before, q_in, lead, short_filter, taps, residue, rate, fwd, inv)

    return project(product, lax.all_gather(out_weight, "ctx", axis=1, tiled=True))


def solution(mesh):
    in_specs = (
        P("ctx", "mp"),
        P("ctx", "mp"),
        P("ctx", "mp"),
        P(None, None, "mp"),
        P(None, "mp"),
        P(None, "mp"),
        P(None, "mp"),
        P("mp", "ctx"),
    )
    out_specs = P("ctx", "mp")
    return jax.shard_map(local, mesh=mesh, in_specs=in_specs, out_specs=out_specs, check_vma=False)
```
